32 devices in a mesh: cells: 4 (over x, core), modes: 8 (over z, y).
Axes of the slice: x: 2, y: 2, z: 4, core: 2. Of those that a mesh axis runs over, the one named last changes fastest.
Arguments:
- hermite_coefficient_array: float32 [8, 64, 32, 2048], P('cells', None, None, 'modes'), may hold values from -6 to 6
- encounter_kernel_array: bfloat16 [14400, 120], replicated, may hold values from -0.046875 to 0.046875
- obstacle_indicator: int32 [8, 64, 32], P('cells'), may hold values 0 or 1
Outputs:
- moments_next: float32 [8, 64, 32, 2048], P('cells', None, None, 'modes')
The draws below stay inside these ranges and needn't reach their ends.
All inputs are finite; a program needn't handle non-finite values. No bound on the sum of `obstacle_indicator` on one device may be relied on, other than what follows from the above.
Results may differ from the reference program's by a relative error of at most 0.0003.
Values sent between devices are 32-bit elements; how exact they have to be, the bound alone decides.
A program may use at most 128 MiB of HBM per device.

```python
import math
import jax
import jax.numpy as jnp
from jax import lax

NY = 64
NZ = 32
MA = 16
MB = 16
MC = 8
LDEG = 7
BASIS_SIZE = 120
MODES = 2048
NX = 8


def plant(array, own_key, smallest, largest):
    extent = array.shape
    index_at = [jax.random.randint(jax.random.fold_in(own_key, axis), (), 0, extent[axis]) for axis in range(len(extent))]
    array = array.at[tuple(index_at)].set(smallest)
    longest = extent.index(max(extent))
    index_at[longest] = (index_at[longest] + 1) % extent[longest]
    return array.at[tuple(index_at)].set(largest)


def block_levels(own_key, dims, shards, least, high):
    level, own = 1.0, jax.random.fold_in(own_key, 6)
    for position, parts in shards:
        heights = jnp.exp(jax.random.uniform(jax.random.fold_in(own, position), (parts,), jnp.float32, least / len(shards), high / len(shards)))
        level = level * jnp.repeat(heights, dims[position] // parts).reshape([-1 if axis == position else 1 for axis in range(len(dims))])
    return level


def normal_values(key, shape, deviation, limit, shards=(), held_as=jnp.bfloat16):
    entries = deviation * jax.random.normal(key, shape, jnp.float32)
    if shards:
        entries = entries * block_levels(key, shape, shards, -0.22, 0.18)
    return jnp.clip(entries, -limit, limit).astype(held_as)


def setup_inputs(seed: int = 0) -> dict:
    key_list = jax.random.split(jax.random.key(seed), 4)
    return {
        "hermite_coefficient_array": normal_values(key_list[0], (NX, NY, NZ, MODES), 1.0, 6.0, ((0, 4), (3, 8)), jnp.float32),
        "encounter_kernel_array": normal_values(key_list[1], (BASIS_SIZE * BASIS_SIZE, BASIS_SIZE), (BASIS_SIZE * BASIS_SIZE) ** -0.5, 0.046875),
        "obstacle_indicator": plant((jax.random.randint(key_list[2], (NX, NY, NZ), 0, 8) < 1).astype(jnp.int32), jax.random.fold_in(key_list[2], 1), 0, 1),
    }


CFL = 0.04
DTC = 0.2

def ladder_ref(field, axis):
    count = field.shape[axis]
    pad_spec = [(0, 0)] * field.ndim
    pad_spec[axis] = (1, 1)
    padded = jnp.pad(field, pad_spec)
    lower_part = lax.slice_in_dim(padded, 0, count, axis=axis)
    upper_part = lax.slice_in_dim(padded, 2, count + 2, axis=axis)
    shape_list = [1] * field.ndim
    shape_list[axis] = count
    level = jnp.arange(count, dtype=jnp.float32).reshape(shape_list)
    return jnp.sqrt(level) * lower_part + jnp.sqrt(level + 1.0) * upper_part

def transport(grid, obstacle_indicator):
    speed_x = 2.0 * math.sqrt(MA)
    speed_y = 2.0 * math.sqrt(MB)
    speed_z = 2.0 * math.sqrt(MC)

    def plane(plane_index):
        center = lax.dynamic_index_in_dim(grid, plane_index, 0, keepdims=False)
        behind = lax.dynamic_index_in_dim(grid, jnp.mod(plane_index - 1, NX), 0, keepdims=False)
        beyond = lax.dynamic_index_in_dim(grid, jnp.mod(plane_index + 1, NX), 0, keepdims=False)
        solid = lax.dynamic_index_in_dim(obstacle_indicator, plane_index, 0, keepdims=False)
        first_axis_gradient = beyond - behind
        lap_x = beyond - 2.0 * center + behind
        next_y = jnp.roll(center, -1, 0)
        prev_y = jnp.roll(center, 1, 0)
        next_z = jnp.roll(center, -1, 1)
        prev_z = jnp.roll(center, 1, 1)
        diff_y = next_y - prev_y
        lap_y = next_y - 2.0 * center + prev_y
        diff_z = next_z - prev_z
        lap_z = next_z - 2.0 * center + prev_z
        shaped = (NY, NZ, MA, MB, MC)
        flux = ladder_ref(first_axis_gradient.reshape(shaped), 2) + ladder_ref(diff_y.reshape(shaped), 3) + ladder_ref(diff_z.reshape(shaped), 4)
        flux = flux.reshape(NY, NZ, MODES)
        update = center + CFL * (-0.5 * flux + 0.5 * (speed_x * lap_x + speed_y * lap_y + speed_z * lap_z))
        return jnp.where(solid[..., None] != 0, center, update)
    return lax.map(plane, jnp.arange(NX, dtype=jnp.int32))

def reference(hermite_coefficient_array, encounter_kernel_array, obstacle_indicator):
    grid = hermite_coefficient_array
    for repeat in range(2):
        grid = transport(grid, obstacle_indicator)
    rows = grid.reshape(NX * NY * NZ, MODES)
    mode_index = jnp.arange(MODES, dtype=jnp.int32)
    degree = mode_index // (MB * MC) + mode_index // MC % MB + mode_index % MC
    low_index = jnp.nonzero(degree <= LDEG, size=BASIS_SIZE)[0].astype(jnp.int32)
    low = rows[:, low_index]

    def collide(block_rows):
        quadratic_factors = (block_rows[:, :, None] * block_rows[:, None, :]).reshape(block_rows.shape[0], BASIS_SIZE * BASIS_SIZE).astype(jnp.bfloat16)
        return jnp.dot(quadratic_factors, encounter_kernel_array, preferred_element_type=jnp.float32)
    scattered_state = lax.map(collide, low.reshape(-1, 512, BASIS_SIZE)).reshape(-1, BASIS_SIZE)
    rows = rows.at[:, low_index].add(DTC * scattered_state)
    return rows.reshape(NX, NY, NZ, MODES)
```

```python
import functools
import math

import jax
import jax.numpy as jnp
import numpy as np
from jax import lax
from jax.experimental import pallas as pl
from jax.experimental.pallas import tpu as pltpu
from jax.sharding import PartitionSpec as P

MA = 16
MB = 16
MC = 8
LDEG = 7
BASIS_SIZE = 120
MODES = 2048
BLOCK = MB * MC
WIDE = 128
GROUP = 16
ROWS = 2
LEAD = 5

CFL = 0.04
DTC = 0.2
MESH = pl.DeviceIdType.MESH


def split3(x):
    hi = x.astype(jnp.bfloat16)
    rest = x - hi.astype(jnp.float32)
    mid = rest.astype(jnp.bfloat16)
    low = (rest - mid.astype(jnp.float32)).astype(jnp.bfloat16)
    return hi, mid, low


def dot(a, b):
    return jnp.dot(a, b, preferred_element_type=jnp.float32)


def loop(lo, hi, f):
    def step(i, carry):
        f(i)
        return carry

    lax.fori_loop(lo, hi, step, 0)


def kernel(cfg, hin, solid, rank, raw, out, f0, f1, tr, xh1, xh2, zh1, zh2, de1, de2,
           mask, coef, sel, sel_t, lx, lr, rx, rr, table, lt, rt, raw_sem, loc_sem, swap_s, swap_r,
           x1_s, x1_r, x2_s, x2_r, z1_s, z1_r, z2_s, z2_r, low_s, low_r, rate_s, rate_r, back_s, back_r, keep_sem):
    planes, rows_y, rows_z, local, nc, nm, ns = cfg
    per = local // BLOCK
    levels = 2 * per
    half = rows_y // 2
    ext = half + 4
    nq = nm // 2
    chunks = half // ROWS
    cells = planes * ROWS * rows_z

    c = lax.axis_index("cells")
    m = lax.axis_index("modes")
    p = lax.rem(m, 2)
    q = lax.div(m, 2)
    other = 1 - p
    mate = (c, q * 2 + other)
    before = (lax.rem(c + nc - 1, nc), m)
    after = (lax.rem(c + 1, nc), m)
    below = (c, m - 2)
    above = (c, m + 2)
    has_below = q > 0
    has_above = q < nq - 1
    is_source = q < ns

    def peer(d):
        return (c, lax.rem(q + d, ns) * 2 + p)

    barrier = pltpu.get_barrier_semaphore()

    def greet(dev):
        pl.semaphore_signal(barrier, inc=1, device_id=dev, device_id_type=MESH)

    for dev in (mate, before, after):
        greet(dev)

    @pl.when(has_below)
    def _():
        greet(below)

    @pl.when(has_above)
    def _():
        greet(above)

    @pl.when(is_source)
    def _():
        for d in range(1, ns):
            greet(peer(d))

    def grid_row(side, e):
        return lax.rem(side * half + (rows_y - 2) + e, rows_y)

    own_pieces = [(0, 2), (2, half + 2), (half + 2, ext)]

    def own(i):
        lo, hi = own_pieces[i]
        return pltpu.make_async_copy(
            hin.at[:, pl.ds(grid_row(p, lo), hi - lo)],
            f0.at[p, :, pl.ds(lo, hi - lo)],
            loc_sem.at[i],
        )

    for i in range(len(own_pieces)):
        own(i).start()
    raw_copy = pltpu.make_async_copy(raw, table, raw_sem)

    greeted = 3 + has_below.astype(jnp.int32) + has_above.astype(jnp.int32)
    pl.semaphore_wait(barrier, greeted + (ns - 1) * is_source.astype(jnp.int32))

    def remote(src, dst, s, r, dev):
        return pltpu.make_async_remote_copy(
            src_ref=src, dst_ref=dst, send_sem=s, recv_sem=r, device_id=dev, device_id_type=MESH
        )

    arrivals = ext // ROWS
    first = chunks + 1

    def rows0(k):
        return pl.ds(k * ROWS, ROWS)

    def rows1(i):
        return pl.ds(i * ROWS + 1, ROWS)

    def rows2(j):
        return pl.ds(j * ROWS + 2, ROWS)

    def swap(k):
        where = pl.ds(grid_row(other, k * ROWS), ROWS)
        return remote(hin.at[:, where], f0.at[p, :, rows0(k)], swap_s.at[k], swap_r.at[k], mate)

    def swap_in(k):
        where = pl.ds(grid_row(other, k * ROWS), ROWS)
        return remote(hin.at[:, where], f0.at[other, :, rows0(k)], swap_s.at[k], swap_r.at[k], mate)

    def edge(field, halo, ss, rs, blk, k, slot, where):
        up = remote(field.at[blk, planes - 1, where], halo.at[0, blk, where],
                    ss.at[0, slot, k], rs.at[0, slot, k], after)
        down = remote(field.at[blk, 0, where], halo.at[1, blk, where],
                      ss.at[1, slot, k], rs.at[1, slot, k], before)
        return up, down

    def edge1(slot, i):
        return edge(f0, xh1, x1_s, x1_r, (p, other)[slot], i, slot, rows1(i))

    def edge2(blk, j):
        return edge(f1, xh2, x2_s, x2_r, blk, j, blk, rows2(j))

    def lanes(j):
        return pl.ds((j % per) * BLOCK, BLOCK)

    def gradient(field, halo, pln, e, j):
        blk = j // per
        nxt = halo[1, blk, e, :, lanes(j)] if pln == planes - 1 else field[blk, pln + 1, e, :, lanes(j)]
        prv = halo[0, blk, e, :, lanes(j)] if pln == 0 else field[blk, pln - 1, e, :, lanes(j)]
        return nxt, prv

    def slopes(field, halo, de, lo):
        def row(r):
            e = lo + r
            for pln in range(planes):
                nxt, prv = gradient(field, halo, pln, e, 0)
                de[0, pln, e] = nxt - prv
                nxt, prv = gradient(field, halo, pln, e, levels - 1)
                de[1, pln, e] = nxt - prv

        loop(0, ROWS, row)

    def to_below(de, zh, ss, rs, k, where):
        return remote(de.at[0, :, where], zh.at[1, :, where], ss.at[0, k], rs.at[0, k], below)

    def to_above(de, zh, ss, rs, k, where):
        return remote(de.at[1, :, where], zh.at[0, :, where], ss.at[1, k], rs.at[1, k], above)

    def z_start(*a):
        @pl.when(has_below)
        def _():
            to_below(*a).start()

        @pl.when(has_above)
        def _():
            to_above(*a).start()

    def z_arrived(*a):
        @pl.when(has_below)
        def _():
            to_above(*a).wait_recv()

        @pl.when(has_above)
        def _():
            to_below(*a).wait_recv()

    def z_sent(*a):
        @pl.when(has_below)
        def _():
            to_below(*a).wait_send()

        @pl.when(has_above)
        def _():
            to_above(*a).wait_send()

    def z1(i):
        return de1, zh1, z1_s, z1_r, i, rows1(i)

    def z2(j):
        return de2, zh2, z2_s, z2_r, j, rows2(j)

    wx = 0.5 * 2.0 * math.sqrt(MA)
    wy = 0.5 * 2.0 * math.sqrt(MB)
    wz = 0.5 * 2.0 * math.sqrt(MC)
    wc = 2.0 * (wx + wy + wz)

    def substep(field, halo, zh, dest, lo):
        def row(r):
            e = lo + r
            for pln in range(planes):
                gas = mask[pln, e]
                pairs = [gradient(field, halo, pln, e, j) for j in range(levels)]
                grads = [zh[0, pln, e]] + [a - b for a, b in pairs] + [zh[1, pln, e]]
                for j in range(levels):
                    blk = j // per
                    mid = field[blk, pln, e, :, lanes(j)]
                    ny = field[blk, pln, e + 1, :, lanes(j)]
                    py = field[blk, pln, e - 1, :, lanes(j)]
                    nz = pltpu.roll(mid, rows_z - 1, 0)
                    pz = pltpu.roll(mid, 1, 0)
                    dy = ny - py
                    dz = nz - pz
                    acc = coef[4 + j : 5 + j, :] * grads[j]
                    acc += coef[4 + levels + j : 5 + levels + j, :] * grads[j + 2]
                    acc += coef[0:1, :] * pltpu.roll(dy, MC, 1)
                    acc += coef[1:2, :] * pltpu.roll(dy, BLOCK - MC, 1)
                    acc += coef[2:3, :] * pltpu.roll(dz, 1, 1)
                    acc += coef[3:4, :] * pltpu.roll(dz, BLOCK - 1, 1)
                    acc += wx * (pairs[j][0] + pairs[j][1]) + wy * (ny + py) + wz * (nz + pz) - wc * mid
                    dest[blk, pln, e, :, lanes(j)] = mid + gas * acc

        loop(0, ROWS, row)

    def take_low(j):
        total = jnp.zeros((cells, WIDE), jnp.float32)
        for level in range(levels):
            x = tr[level // per, :, rows2(j), :, lanes(level)].reshape(cells, BLOCK)
            for term in split3(x):
                total += dot(term, sel[level])
        lx[j] = total

    def owner(j):
        return lax.rem(j, ns)

    def distance(j):
        return lax.rem(owner(j) + ns - q, ns)

    def low_send(j):
        return remote(lx.at[j], lr.at[j, distance(j) - 1], low_s.at[j], low_r.at[j, distance(j) - 1],
                      (c, owner(j) * 2 + p))

    def low_take(j, d):
        return remote(lx.at[j], lr.at[j, d - 1], low_s.at[j], low_r.at[j, d - 1], peer(d))

    def rate_send(j, d):
        return remote(rx.at[j], rr.at[j], rate_s.at[j, d - 1], rate_r.at[j], peer(d))

    def rate_take(j):
        return remote(rx.at[j], rr.at[j], rate_s.at[j, 0], rate_r.at[j], peer(ns - 1))

    def collide(j):
        low = lx[j]
        for d in range(1, ns):
            low = low + lr[j, d - 1]
        lt[...] = low.T
        rt[...] = jnp.zeros_like(rt)

        def step(start, count, columns):
            rows = lt[pl.ds(start, count), :]
            values = lt[0:BASIS_SIZE, :]
            factors = jnp.concatenate(
                [(rows[i : i + 1, :] * values) for i in range(count)], axis=0
            ).astype(jnp.bfloat16)
            rt[0:BASIS_SIZE, :] += dot(table[:, columns], factors)

        def whole(g):
            width = GROUP * BASIS_SIZE
            step(pl.multiple_of(g * GROUP, GROUP), GROUP, pl.ds(pl.multiple_of(g * width, WIDE), width))

        groups = BASIS_SIZE // GROUP
        loop(0, groups, whole)
        if groups * GROUP < BASIS_SIZE:
            step(groups * GROUP, BASIS_SIZE - groups * GROUP,
                 pl.ds(groups * GROUP * BASIS_SIZE, (BASIS_SIZE - groups * GROUP) * BASIS_SIZE))
        rx[j] = rt[...].T

    def lift(j, rates):
        terms = split3(rates)
        for level in range(levels):
            add = sum(dot(term, sel_t[level]) for term in terms) * DTC
            tr[level // per, :, rows2(j), :, lanes(level)] += add.reshape(planes, ROWS, rows_z, BLOCK)

    def give_back(j):
        return remote(tr.at[other, :, rows2(j)], out.at[:, pl.ds(p * half + j * ROWS, ROWS)],
                      back_s.at[j], back_r.at[j], mate)

    def got_back(j):
        return remote(tr.at[other, :, rows2(j)], out.at[:, pl.ds(other * half + j * ROWS, ROWS)],
                      back_s.at[j], back_r.at[j], mate)

    def keep(j):
        return pltpu.make_async_copy(tr.at[p, :, rows2(j)], out.at[:, pl.ds(p * half + j * ROWS, ROWS)],
                                     keep_sem.at[j])

    def finish(j):
        give_back(j).start()
        keep(j).start()

    def start_all(copies):
        for copy in copies:
            copy.start()

    def during(index, count, f):
        @pl.when(jnp.logical_and(index >= 0, index < count))
        def _():
            f(index)

    loop(0, 2, lambda k: swap(k).start())
    for i in range(len(own_pieces)):
        own(i).wait()
    loop(0, min(LEAD, first), lambda i: start_all(edge1(0, i)))
    loop(2, arrivals, lambda k: swap(k).start())

    @pl.when(is_source)
    def _():
        raw_copy.start()

    @pl.when(q == 0)
    def _():
        for zh in (zh1, zh2):
            zh[0] = jnp.zeros_like(zh[0])

    @pl.when(q == nq - 1)
    def _():
        for zh in (zh1, zh2):
            zh[1] = jnp.zeros_like(zh[1])

    lane = lax.broadcasted_iota(jnp.int32, (1, BLOCK), 1)
    lane_b, lane_c = lax.div(lane, MC), lax.rem(lane, MC)

    def low_root(x):
        return -0.5 * jnp.sqrt(x.astype(jnp.float32))

    def high_root(x, count):
        return jnp.where(x + 1 < count, -0.5 * jnp.sqrt((x + 1).astype(jnp.float32)), 0.0)

    coef[0:1] = low_root(lane_b)
    coef[1:2] = high_root(lane_b, MB)
    coef[2:3] = low_root(lane_c)
    coef[3:4] = high_root(lane_c, MC)
    wide = lax.broadcasted_iota(jnp.int32, (WIDE, BLOCK), 0)
    for j in range(levels):
        level = q * levels + j
        coef[4 + j : 5 + j] = low_root(0 * lane + level)
        coef[4 + levels + j : 5 + levels + j] = high_root(0 * lane + level, MA)
        mine = jnp.where(rank[pl.ds(level, 1), :] == wide, 1.0, 0.0)
        sel_t[j] = mine.astype(jnp.bfloat16)
        sel[j] = mine.T.astype(jnp.bfloat16)

    clear = [jnp.where(solid[pln] != 0, 0.0, 1.0).astype(jnp.bfloat16) for pln in range(planes)]
    line = lax.broadcasted_iota(jnp.int32, (rows_y, BLOCK), 0)

    def spread(e):
        pick = jnp.where(line == grid_row(p, e), 1.0, 0.0).astype(jnp.bfloat16)
        for pln in range(planes):
            mask[pln, e] = dot(clear[pln], pick) * CFL

    loop(1, ext - 1, spread)

    def advance(t):
        def arrive(i):
            @pl.when(i == 0)
            def _():
                swap_in(0).wait_recv()

            swap_in(i + 1).wait_recv()
            start_all(edge1(1, i))

            @pl.when(i + LEAD < first)
            def _():
                start_all(edge1(0, i + LEAD))

        def slope1(i):
            for slot in range(2):
                for copy in edge1(slot, i):
                    copy.wait_recv()
            slopes(f0, xh1, de1, i * ROWS + 1)
            z_start(*z1(i))

        def slope2(j):
            for blk in range(2):
                for copy in edge2(blk, j):
                    copy.wait_recv()
            slopes(f1, xh2, de2, j * ROWS + 2)
            z_start(*z2(j))

        def move1(i):
            z_arrived(*z1(i))
            substep(f0, xh1, zh1, f1, i * ROWS + 1)

            @pl.when(i >= 1)
            def _():
                for blk in range(2):
                    start_all(edge2(blk, i - 1))

        def move2(j):
            z_arrived(*z2(j))
            substep(f1, xh2, zh2, tr, j * ROWS + 2)

            @pl.when(is_source)
            def _():
                take_low(j)

                @pl.when(q != owner(j))
                def _():
                    low_send(j).start()

            @pl.when(jnp.logical_not(is_source))
            def _():
                finish(j)

        def meet(j):
            @pl.when(jnp.logical_and(is_source, q == owner(j)))
            def _():
                for d in range(1, ns):
                    low_take(j, d).wait_recv()
                collide(j)
                for d in range(1, ns):
                    rate_send(j, d).start()
                lift(j, rx[j])
                finish(j)

        def settle(j):
            @pl.when(jnp.logical_and(is_source, q != owner(j)))
            def _():
                rate_take(j).wait_recv()
                lift(j, rr[j])
                finish(j)

        during(t, first, arrive)
        during(t - 2, first, slope1)
        during(t - 6, chunks, slope2)
        during(t - 3, first, move1)
        during(t - 7, chunks, move2)

        @pl.when(jnp.logical_and(is_source, t == 8))
        def _():
            raw_copy.wait()

        during(t - 8, chunks, meet)
        during(t - 10, chunks, settle)

    loop(0, chunks + 11, advance)

    def drain1(i):
        z_sent(*z1(i))
        for slot in range(2):
            for copy in edge1(slot, i):
                copy.wait_send()

    def drain2(j):
        z_sent(*z2(j))
        for blk in range(2):
            for copy in edge2(blk, j):
                copy.wait_send()

        @pl.when(jnp.logical_and(is_source, q == owner(j)))
        def _():
            for d in range(1, ns):
                rate_send(j, d).wait_send()

        @pl.when(jnp.logical_and(is_source, q != owner(j)))
        def _():
            low_send(j).wait_send()

    loop(0, arrivals, lambda k: swap(k).wait_send())
    loop(0, first, drain1)
    loop(0, chunks, drain2)

    def drain3(j):
        keep(j).wait()
        give_back(j).wait_send()
        got_back(j).wait_recv()

    loop(0, chunks, drain3)


def body(hermite_coefficient_array, encounter_kernel_array, obstacle_indicator):
    planes, rows_y, rows_z, local = hermite_coefficient_array.shape
    nc = lax.axis_size("cells")
    nm = lax.axis_size("modes")
    per = local // BLOCK
    levels = 2 * per
    half = rows_y // 2
    ns = -(-(LDEG + 1) // levels)
    chunks = half // ROWS
    ext = half + 4

    index = np.arange(MODES)
    flags = (index // BLOCK + index // MC % MB + index % MC <= LDEG).astype(np.int32)
    rank = jnp.asarray(np.where(flags == 1, np.cumsum(flags) - 1, -1).reshape(MA, BLOCK), jnp.int32)

    peers = max(ns - 1, 1)
    cells = planes * ROWS * rows_z
    field = pltpu.VMEM((2, planes, ext, rows_z, local), jnp.float32)
    halo = pltpu.VMEM((2, 2, ext, rows_z, local), jnp.float32)
    slope = pltpu.VMEM((2, planes, ext, rows_z, BLOCK), jnp.float32)
    dma = pltpu.SemaphoreType.DMA
    cfg = (planes, rows_y, rows_z, local, nc, nm, ns)
    vmem = pl.BlockSpec(memory_space=pltpu.VMEM)
    anywhere = pl.BlockSpec(memory_space=pl.ANY)
    return pl.pallas_call(
        functools.partial(kernel, cfg),
        out_shape=pltpu.VMEM(hermite_coefficient_array.shape, jnp.float32),
        in_specs=[anywhere, vmem, vmem, anywhere],
        out_specs=vmem,
        scratch_shapes=[
            field, field, field, halo, halo, slope, slope, slope, slope,
            pltpu.VMEM((planes, ext, rows_z, BLOCK), jnp.float32),
            pltpu.VMEM((4 + 2 * levels + -(4 + 2 * levels) % 8, BLOCK), jnp.float32),
            pltpu.VMEM((levels, BLOCK, WIDE), jnp.bfloat16),
            pltpu.VMEM((levels, WIDE, BLOCK), jnp.bfloat16),
            pltpu.VMEM((chunks, cells, WIDE), jnp.float32),
            pltpu.VMEM((chunks, peers, cells, WIDE), jnp.float32),
            pltpu.VMEM((chunks, cells, WIDE), jnp.float32),
            pltpu.VMEM((chunks, cells, WIDE), jnp.float32),
            pltpu.VMEM((BASIS_SIZE, BASIS_SIZE * BASIS_SIZE), jnp.bfloat16),
            pltpu.VMEM((WIDE, cells), jnp.float32),
            pltpu.VMEM((WIDE, cells), jnp.float32),
            dma, dma((3,)), dma((ext // ROWS,)), dma((ext // ROWS,)),
            dma((2, 2, chunks + 1)), dma((2, 2, chunks + 1)), dma((2, 2, chunks)), dma((2, 2, chunks)),
            dma((2, chunks + 1)), dma((2, chunks + 1)), dma((2, chunks)), dma((2, chunks)),
            dma((chunks,)), dma((chunks, peers)), dma((chunks, peers)), dma((chunks,)),
            dma((chunks,)), dma((chunks,)), dma((chunks,)),
        ],
        compiler_params=pltpu.CompilerParams(
            collective_id=0, has_side_effects=True, vmem_limit_bytes=54 * 1024 * 1024
        ),
    )(hermite_coefficient_array, obstacle_indicator.transpose(0, 2, 1), rank, encounter_kernel_array.T)


def solution(mesh):
    placed = (P("cells", None, None, "modes"), P(), P("cells", None, None))
    return jax.shard_map(
        body, mesh=mesh, in_specs=placed, out_specs=P("cells", None, None, "modes"), check_vma=False
    )
```

```python
import functools
import math

import jax
import jax.numpy as jnp
import numpy as np
from jax import lax
from jax.experimental import pallas as pl
from jax.experimental.pallas import tpu as pltpu
from jax.sharding import PartitionSpec as P

MA = 16
MB = 16
MC = 8
LDEG = 7
BASIS_SIZE = 120
MODES = 2048
BLOCK = MB * MC
WIDE = 128
GROUP = 64
ROWS = 2
LEAD = 5

CFL = 0.04
DTC = 0.2
MESH = pl.DeviceIdType.MESH


def split3(x):
    hi = x.astype(jnp.bfloat16)
    rest = x - hi.astype(jnp.float32)
    mid = rest.astype(jnp.bfloat16)
    low = (rest - mid.astype(jnp.float32)).astype(jnp.bfloat16)
    return hi, mid, low


def dot(a, b):
    return jnp.dot(a, b, preferred_element_type=jnp.float32)


def loop(lo, hi, f):
    def step(i, carry):
        f(i)
        return carry

    lax.fori_loop(lo, hi, step, 0)


def kernel(cfg, hin, solid, rank, raw, out, f0, f1, tr, xh1, xh2, zh1, zh2, de1, de2,
           mask, coef, sel, sel_t, lx, lr, rx, rr, table, lt, rt, raw_sem, loc_sem, swap_s, swap_r,
           x1_s, x1_r, x2_s, x2_r, z1_s, z1_r, z2_s, z2_r, low_s, rate_s, meet_r, back_s, back_r, keep_sem):
    planes, rows_y, rows_z, local, nc, nm, ns = cfg
    per = local // BLOCK
    levels = 2 * per
    half = rows_y // 2
    ext = half + 4
    nq = nm // 2
    chunks = half // ROWS
    cells = planes * ROWS * rows_z

    c = lax.axis_index("cells")
    m = lax.axis_index("modes")
    p = lax.rem(m, 2)
    q = lax.div(m, 2)
    other = 1 - p
    mate = (c, q * 2 + other)
    before = (lax.rem(c + nc - 1, nc), m)
    after = (lax.rem(c + 1, nc), m)
    below = (c, m - 2)
    above = (c, m + 2)
    has_below = q > 0
    has_above = q < nq - 1
    is_source = q < ns

    def peer(d):
        return (c, lax.rem(q + d, ns) * 2 + p)

    barrier = pltpu.get_barrier_semaphore()

    def greet(dev):
        pl.semaphore_signal(barrier, inc=1, device_id=dev, device_id_type=MESH)

    for dev in (mate, before, after):
        greet(dev)

    @pl.when(has_below)
    def _():
        greet(below)

    @pl.when(has_above)
    def _():
        greet(above)

    @pl.when(is_source)
    def _():
        for d in range(1, ns):
            greet(peer(d))

    def grid_row(side, e):
        return lax.rem(side * half + (rows_y - 2) + e, rows_y)

    own_pieces = [(0, 2), (2, half + 2), (half + 2, ext)]

    def own(i):
        lo, hi = own_pieces[i]
        return pltpu.make_async_copy(
            hin.at[:, pl.ds(grid_row(p, lo), hi - lo)],
            f0.at[p, :, pl.ds(lo, hi - lo)],
            loc_sem,
        )

    for i in range(len(own_pieces)):
        own(i).start()
    raw_copy = pltpu.make_async_copy(raw, table, raw_sem)

    greeted = 3 + has_below.astype(jnp.int32) + has_above.astype(jnp.int32)
    pl.semaphore_wait(barrier, greeted + (ns - 1) * is_source.astype(jnp.int32))

    def remote(src, dst, s, r, dev):
        return pltpu.make_async_remote_copy(
            src_ref=src, dst_ref=dst, send_sem=s, recv_sem=r, device_id=dev, device_id_type=MESH
        )

    arrivals = ext // ROWS
    first = chunks + 1

    def rows0(k):
        return pl.ds(k * ROWS, ROWS)

    def rows1(i):
        return pl.ds(i * ROWS + 1, ROWS)

    def rows2(j):
        return pl.ds(j * ROWS + 2, ROWS)

    def swap(k):
        where = pl.ds(grid_row(other, k * ROWS), ROWS)
        return remote(hin.at[:, where], f0.at[p, :, rows0(k)], swap_s, swap_r.at[k], mate)

    def swap_in(k):
        where = pl.ds(grid_row(other, k * ROWS), ROWS)
        return remote(hin.at[:, where], f0.at[other, :, rows0(k)], swap_s, swap_r.at[k], mate)

    def edge(field, halo, ss, rs, blk, k, where):
        up = remote(field.at[blk, planes - 1, where], halo.at[0, blk, where], ss, rs.at[k], after)
        down = remote(field.at[blk, 0, where], halo.at[1, blk, where], ss, rs.at[k], before)
        return up, down

    def edge1(slot, i):
        return edge(f0, xh1, x1_s, x1_r, (p, other)[slot], i, rows1(i))

    def edge2(blk, j):
        return edge(f1, xh2, x2_s, x2_r, blk, j, rows2(j))

    def whole(ref, s, r):
        return remote(ref, ref, s, r, mate)

    def lanes(j):
        return pl.ds((j % per) * BLOCK, BLOCK)

    def gradient(field, halo, pln, e, j):
        blk = j // per
        nxt = halo[1, blk, e, :, lanes(j)] if pln == planes - 1 else field[blk, pln + 1, e, :, lanes(j)]
        prv = halo[0, blk, e, :, lanes(j)] if pln == 0 else field[blk, pln - 1, e, :, lanes(j)]
        return nxt, prv

    def slopes(field, halo, de, lo):
        def row(r):
            e = lo + r
            for pln in range(planes):
                nxt, prv = gradient(field, halo, pln, e, 0)
                de[0, pln, e] = nxt - prv
                nxt, prv = gradient(field, halo, pln, e, levels - 1)
                de[1, pln, e] = nxt - prv

        loop(0, ROWS, row)

    def to_below(de, zh, ss, rs, k, where):
        return remote(de.at[0, :, where], zh.at[1, :, where], ss, rs.at[k], below)

    def to_above(de, zh, ss, rs, k, where):
        return remote(de.at[1, :, where], zh.at[0, :, where], ss, rs.at[k], above)

    def z_start(*a):
        @pl.when(has_below)
        def _():
            to_below(*a).start()

        @pl.when(has_above)
        def _():
            to_above(*a).start()

    inner = jnp.logical_and(has_below, has_above)
    outer = jnp.logical_xor(has_below, has_above)

    def z_arrived(de, zh, ss, rs, k, where):
        @pl.when(inner)
        def _():
            whole(zh.at[:, :, where], ss, rs.at[k]).wait_recv()

        @pl.when(outer)
        def _():
            whole(zh.at[0, :, where], ss, rs.at[k]).wait_recv()

    def z_sent(de, ss, where):
        @pl.when(inner)
        def _():
            whole(de.at[:, :, where], ss, ss).wait_send()

        @pl.when(outer)
        def _():
            whole(de.at[0, :, where], ss, ss).wait_send()

    def z1(i):
        return de1, zh1, z1_s, z1_r, i, rows1(i)

    def z2(j):
        return de2, zh2, z2_s, z2_r, j, rows2(j)

    wx = 0.5 * 2.0 * math.sqrt(MA)
    wy = 0.5 * 2.0 * math.sqrt(MB)
    wz = 0.5 * 2.0 * math.sqrt(MC)
    wc = 2.0 * (wx + wy + wz)

    def substep(field, halo, zh, dest, lo):
        def row(r):
            e = lo + r
            for pln in range(planes):
                gas = mask[pln, e]
                pairs = [gradient(field, halo, pln, e, j) for j in range(levels)]
                grads = [zh[0, pln, e]] + [a - b for a, b in pairs] + [zh[1, pln, e]]
                for j in range(levels):
                    blk = j // per
                    mid = field[blk, pln, e, :, lanes(j)]
                    ny = field[blk, pln, e + 1, :, lanes(j)]
                    py = field[blk, pln, e - 1, :, lanes(j)]
                    nz = pltpu.roll(mid, rows_z - 1, 0)
                    pz = pltpu.roll(mid, 1, 0)
                    dy = ny - py
                    dz = nz - pz
                    acc = coef[4 + j : 5 + j, :] * grads[j]
                    acc += coef[4 + levels + j : 5 + levels + j, :] * grads[j + 2]
                    acc += coef[0:1, :] * pltpu.roll(dy, MC, 1)
                    acc += coef[1:2, :] * pltpu.roll(dy, BLOCK - MC, 1)
                    acc += coef[2:3, :] * pltpu.roll(dz, 1, 1)
                    acc += coef[3:4, :] * pltpu.roll(dz, BLOCK - 1, 1)
                    acc += wx * (pairs[j][0] + pairs[j][1]) + wy * (ny + py) + wz * (nz + pz) - wc * mid
                    dest[blk, pln, e, :, lanes(j)] = mid + gas * acc

        loop(0, ROWS, row)

    def take_low(j):
        total = jnp.zeros((cells, WIDE), jnp.float32)
        for level in range(levels):
            x = tr[level // per, :, rows2(j), :, lanes(level)].reshape(cells, BLOCK)
            for term in split3(x):
                total += dot(term, sel[level])
        lx[j] = total

    def owner(j):
        return lax.rem(j, ns)

    def distance(j):
        return lax.rem(owner(j) + ns - q, ns)

    def low_send(j):
        return remote(lx.at[j], lr.at[j, distance(j) - 1], low_s, meet_r.at[j], (c, owner(j) * 2 + p))

    def rate_send(j, d):
        return remote(rx.at[j], rr.at[j], rate_s, meet_r.at[j], peer(d))

    def collide(j):
        low = lx[j]
        for d in range(1, ns):
            low = low + lr[j, d - 1]
        lt[...] = low.T
        rt[...] = jnp.zeros_like(rt)

        def step(start, count, columns):
            rows = lt[pl.ds(start, count), :]
            values = lt[0:BASIS_SIZE, :]
            factors = jnp.concatenate(
                [(rows[i : i + 1, :] * values) for i in range(count)], axis=0
            ).astype(jnp.bfloat16)
            rt[0:BASIS_SIZE, :] += dot(table[:, columns], factors)

        def block(g):
            width = GROUP * BASIS_SIZE
            step(pl.multiple_of(g * GROUP, GROUP), GROUP, pl.ds(pl.multiple_of(g * width, WIDE), width))

        groups = BASIS_SIZE // GROUP
        loop(0, groups, block)
        if groups * GROUP < BASIS_SIZE:
            step(groups * GROUP, BASIS_SIZE - groups * GROUP,
                 pl.ds(groups * GROUP * BASIS_SIZE, (BASIS_SIZE - groups * GROUP) * BASIS_SIZE))
        rx[j] = rt[...].T

    def lift(j, rates):
        terms = split3(rates)
        for level in range(levels):
            add = sum(dot(term, sel_t[level]) for term in terms) * DTC
            tr[level // per, :, rows2(j), :, lanes(level)] += add.reshape(planes, ROWS, rows_z, BLOCK)

    def give_back(j):
        return remote(tr.at[other, :, rows2(j)], out.at[:, pl.ds(p * half + j * ROWS, ROWS)],
                      back_s, back_r, mate)

    def keep(j):
        return pltpu.make_async_copy(tr.at[p, :, rows2(j)], out.at[:, pl.ds(p * half + j * ROWS, ROWS)],
                                     keep_sem)

    def finish(j):
        give_back(j).start()
        keep(j).start()

    def start_all(copies):
        for copy in copies:
            copy.start()

    def during(index, count, f):
        @pl.when(jnp.logical_and(index >= 0, index < count))
        def _():
            f(index)

    loop(0, 2, lambda k: swap(k).start())
    pltpu.make_async_copy(f0.at[p], f0.at[p], loc_sem).wait()
    loop(0, min(LEAD, first), lambda i: start_all(edge1(0, i)))
    loop(2, arrivals, lambda k: swap(k).start())

    @pl.when(is_source)
    def _():
        raw_copy.start()

    @pl.when(q == 0)
    def _():
        for zh in (zh1, zh2):
            zh[0] = jnp.zeros_like(zh[0])

    @pl.when(q == nq - 1)
    def _():
        for zh in (zh1, zh2):
            zh[1] = jnp.zeros_like(zh[1])

    lane = lax.broadcasted_iota(jnp.int32, (1, BLOCK), 1)
    lane_b, lane_c = lax.div(lane, MC), lax.rem(lane, MC)

    def low_root(x):
        return -0.5 * jnp.sqrt(x.astype(jnp.float32))

    def high_root(x, count):
        return jnp.where(x + 1 < count, -0.5 * jnp.sqrt((x + 1).astype(jnp.float32)), 0.0)

    coef[0:1] = low_root(lane_b)
    coef[1:2] = high_root(lane_b, MB)
    coef[2:3] = low_root(lane_c)
    coef[3:4] = high_root(lane_c, MC)
    wide = lax.broadcasted_iota(jnp.int32, (WIDE, BLOCK), 0)
    for j in range(levels):
        level = q * levels + j
        coef[4 + j : 5 + j] = low_root(0 * lane + level)
        coef[4 + levels + j : 5 + levels + j] = high_root(0 * lane + level, MA)
        mine = jnp.where(rank[pl.ds(level, 1), :] == wide, 1.0, 0.0)
        sel_t[j] = mine.astype(jnp.bfloat16)
        sel[j] = mine.T.astype(jnp.bfloat16)

    clear = [jnp.where(solid[pln] != 0, 0.0, 1.0).astype(jnp.bfloat16) for pln in range(planes)]
    line = lax.broadcasted_iota(jnp.int32, (rows_y, BLOCK), 0)

    def spread(e):
        pick = jnp.where(line == grid_row(p, e), 1.0, 0.0).astype(jnp.bfloat16)
        for pln in range(planes):
            mask[pln, e] = dot(clear[pln], pick) * CFL

    loop(1, ext - 1, spread)

    def advance(t):
        def arrive(i):
            @pl.when(i == 0)
            def _():
                swap_in(0).wait_recv()

            swap_in(i + 1).wait_recv()
            start_all(edge1(1, i))

            @pl.when(i + LEAD < first)
            def _():
                start_all(edge1(0, i + LEAD))

        def slope1(i):
            whole(xh1.at[:, :, rows1(i)], x1_s, x1_r.at[i]).wait_recv()
            slopes(f0, xh1, de1, i * ROWS + 1)
            z_start(*z1(i))

        def slope2(j):
            whole(xh2.at[:, :, rows2(j)], x2_s, x2_r.at[j]).wait_recv()
            slopes(f1, xh2, de2, j * ROWS + 2)
            z_start(*z2(j))

        def move1(i):
            z_arrived(*z1(i))
            substep(f0, xh1, zh1, f1, i * ROWS + 1)

            @pl.when(i >= 1)
            def _():
                for blk in range(2):
                    start_all(edge2(blk, i - 1))

        def move2(j):
            z_arrived(*z2(j))
            substep(f1, xh2, zh2, tr, j * ROWS + 2)

            @pl.when(is_source)
            def _():
                take_low(j)

                @pl.when(q != owner(j))
                def _():
                    low_send(j).start()

            @pl.when(jnp.logical_not(is_source))
            def _():
                finish(j)

        def meet(j):
            @pl.when(jnp.logical_and(is_source, q == owner(j)))
            def _():
                if ns > 1:
                    whole(lr.at[j], low_s, meet_r.at[j]).wait_recv()
                collide(j)
                for d in range(1, ns):
                    rate_send(j, d).start()
                lift(j, rx[j])
                finish(j)

        def settle(j):
            @pl.when(jnp.logical_and(is_source, q != owner(j)))
            def _():
                whole(rr.at[j], rate_s, meet_r.at[j]).wait_recv()
                lift(j, rr[j])
                finish(j)

        during(t, first, arrive)
        during(t - 2, first, slope1)
        during(t - 6, chunks, slope2)
        during(t - 3, first, move1)
        during(t - 7, chunks, move2)

        @pl.when(jnp.logical_and(is_source, t == 8))
        def _():
            raw_copy.wait()

        during(t - 8, chunks, meet)
        during(t - 10, chunks, settle)

    loop(0, chunks + 11, advance)

    whole(f0.at[p], swap_s, swap_s).wait_send()
    whole(xh1.at[:, :, pl.ds(1, first * ROWS)], x1_s, x1_s).wait_send()
    whole(xh2.at[:, :, pl.ds(2, half)], x2_s, x2_s).wait_send()
    z_sent(de1, z1_s, pl.ds(1, first * ROWS))
    z_sent(de2, z2_s, pl.ds(2, half))
    if ns > 1:
        @pl.when(is_source)
        def _():
            share = chunks // ns
            whole(lx.at[pl.ds(0, chunks - share)], low_s, low_s).wait_send()
            whole(lx.at[pl.ds(0, share * (ns - 1))], rate_s, rate_s).wait_send()

    pltpu.make_async_copy(tr.at[p, :, pl.ds(2, half)], tr.at[p, :, pl.ds(2, half)], keep_sem).wait()
    whole(tr.at[other, :, pl.ds(2, half)], back_s, back_s).wait_send()
    whole(out.at[:, pl.ds(other * half, half)], back_r, back_r).wait_recv()


def body(hermite_coefficient_array, encounter_kernel_array, obstacle_indicator):
    planes, rows_y, rows_z, local = hermite_coefficient_array.shape
    nc = lax.axis_size("cells")
    nm = lax.axis_size("modes")
    per = local // BLOCK
    levels = 2 * per
    half = rows_y // 2
    ns = -(-(LDEG + 1) // levels)
    chunks = half // ROWS
    ext = half + 4

    index = np.arange(MODES)
    flags = (index // BLOCK + index // MC % MB + index % MC <= LDEG).astype(np.int32)
    rank = jnp.asarray(np.where(flags == 1, np.cumsum(flags) - 1, -1).reshape(MA, BLOCK), jnp.int32)

    peers = max(ns - 1, 1)
    cells = planes * ROWS * rows_z
    field = pltpu.VMEM((2, planes, ext, rows_z, local), jnp.float32)
    halo = pltpu.VMEM((2, 2, ext, rows_z, local), jnp.float32)
    slope = pltpu.VMEM((2, planes, ext, rows_z, BLOCK), jnp.float32)
    dma = pltpu.SemaphoreType.DMA
    cfg = (planes, rows_y, rows_z, local, nc, nm, ns)
    vmem = pl.BlockSpec(memory_space=pltpu.VMEM)
    anywhere = pl.BlockSpec(memory_space=pl.ANY)
    return pl.pallas_call(
        functools.partial(kernel, cfg),
        out_shape=pltpu.VMEM(hermite_coefficient_array.shape, jnp.float32),
        in_specs=[anywhere, vmem, vmem, anywhere],
        out_specs=vmem,
        scratch_shapes=[
            field, field, field, halo, halo, slope, slope, slope, slope,
            pltpu.VMEM((planes, ext, rows_z, BLOCK), jnp.float32),
            pltpu.VMEM((4 + 2 * levels + -(4 + 2 * levels) % 8, BLOCK), jnp.float32),
            pltpu.VMEM((levels, BLOCK, WIDE), jnp.bfloat16),
            pltpu.VMEM((levels, WIDE, BLOCK), jnp.bfloat16),
            pltpu.VMEM((chunks, cells, WIDE), jnp.float32),
            pltpu.VMEM((chunks, peers, cells, WIDE), jnp.float32),
            pltpu.VMEM((chunks, cells, WIDE), jnp.float32),
            pltpu.VMEM((chunks, cells, WIDE), jnp.float32),
            pltpu.VMEM((BASIS_SIZE, BASIS_SIZE * BASIS_SIZE), jnp.bfloat16),
            pltpu.VMEM((WIDE, cells), jnp.float32),
            pltpu.VMEM((WIDE, cells), jnp.float32),
            dma, dma, dma, dma((ext // ROWS,)), dma, dma((chunks + 1,)), dma, dma((chunks,)),
            dma, dma((chunks + 1,)), dma, dma((chunks,)), dma, dma, dma((chunks,)), dma, dma, dma,
        ],
        compiler_params=pltpu.CompilerParams(
            collective_id=0, has_side_effects=True, vmem_limit_bytes=54 * 1024 * 1024
        ),
    )(hermite_coefficient_array, obstacle_indicator.transpose(0, 2, 1), rank, encounter_kernel_array.T)


def solution(mesh):
    placed = (P("cells", None, None, "modes"), P(), P("cells", None, None))
    return jax.shard_map(
        body, mesh=mesh, in_specs=placed, out_specs=P("cells", None, None, "modes"), check_vma=False
    )
```

```python
import functools
import math

import jax
import jax.numpy as jnp
import numpy as np
from jax import lax
from jax.experimental import pallas as pl
from jax.experimental.pallas import tpu as pltpu
from jax.sharding import PartitionSpec as P

MA = 16
MB = 16
MC = 8
LDEG = 7
BASIS_SIZE = 120
MODES = 2048
BLOCK = MB * MC
WIDE = 128
GROUP = 64
ROWS = 2
LEAD = 5

CFL = 0.04
DTC = 0.2
MESH = pl.DeviceIdType.MESH


def split3(x):
    hi = x.astype(jnp.bfloat16)
    rest = x - hi.astype(jnp.float32)
    mid = rest.astype(jnp.bfloat16)
    low = (rest - mid.astype(jnp.float32)).astype(jnp.bfloat16)
    return hi, mid, low


def dot(a, b):
    return jnp.dot(a, b, preferred_element_type=jnp.float32)


def loop(lo, hi, f):
    def step(i, carry):
        f(i)
        return carry

    lax.fori_loop(lo, hi, step, 0)


def kernel(cfg, hin, solid, rank, raw, out, f0, f1, tr, xh1, xh2, zh1, zh2, de1, de2,
           mask, coef, sel, sel_t, lx, lr, table, lt, rt, raw_sem, loc_sem, swap_s, swap_r,
           x1_s, x1_r, x2_s, x2_r, z1_s, z1_r, z2_s, z2_r, low_s, meet_r, back_s, back_r, keep_sem):
    planes, rows_y, rows_z, local, nc, nm, spans = cfg
    ns = len(spans)
    per = local // BLOCK
    levels = 2 * per
    half = rows_y // 2
    ext = half + 4
    nq = nm // 2
    chunks = half // ROWS
    cells = planes * ROWS * rows_z

    c = lax.axis_index("cells")
    m = lax.axis_index("modes")
    p = lax.rem(m, 2)
    q = lax.div(m, 2)
    other = 1 - p
    mate = (c, q * 2 + other)
    before = (lax.rem(c + nc - 1, nc), m)
    after = (lax.rem(c + 1, nc), m)
    below = (c, m - 2)
    above = (c, m + 2)
    has_below = q > 0
    has_above = q < nq - 1
    is_source = q < ns

    def peer(d):
        return (c, lax.rem(q + d, ns) * 2 + p)

    barrier = pltpu.get_barrier_semaphore()

    def greet(dev):
        pl.semaphore_signal(barrier, inc=1, device_id=dev, device_id_type=MESH)

    for dev in (mate, before, after):
        greet(dev)

    @pl.when(has_below)
    def _():
        greet(below)

    @pl.when(has_above)
    def _():
        greet(above)

    @pl.when(is_source)
    def _():
        for d in range(1, ns):
            greet(peer(d))

    def grid_row(side, e):
        return lax.rem(side * half + (rows_y - 2) + e, rows_y)

    own_pieces = [(0, 2), (2, half + 2), (half + 2, ext)]

    def own(i):
        lo, hi = own_pieces[i]
        return pltpu.make_async_copy(
            hin.at[:, pl.ds(grid_row(p, lo), hi - lo)],
            f0.at[p, :, pl.ds(lo, hi - lo)],
            loc_sem,
        )

    for i in range(len(own_pieces)):
        own(i).start()
    raw_copy = pltpu.make_async_copy(raw, table, raw_sem)

    greeted = 3 + has_below.astype(jnp.int32) + has_above.astype(jnp.int32)
    pl.semaphore_wait(barrier, greeted + (ns - 1) * is_source.astype(jnp.int32))

    def remote(src, dst, s, r, dev):
        return pltpu.make_async_remote_copy(
            src_ref=src, dst_ref=dst, send_sem=s, recv_sem=r, device_id=dev, device_id_type=MESH
        )

    arrivals = ext // ROWS
    first = chunks + 1

    def rows0(k):
        return pl.ds(k * ROWS, ROWS)

    def rows1(i):
        return pl.ds(i * ROWS + 1, ROWS)

    def rows2(j):
        return pl.ds(j * ROWS + 2, ROWS)

    def swap(k):
        where = pl.ds(grid_row(other, k * ROWS), ROWS)
        return remote(hin.at[:, where], f0.at[p, :, rows0(k)], swap_s, swap_r.at[k], mate)

    def swap_in(k):
        where = pl.ds(grid_row(other, k * ROWS), ROWS)
        return remote(hin.at[:, where], f0.at[other, :, rows0(k)], swap_s, swap_r.at[k], mate)

    def edge(field, halo, ss, rs, blk, k, where):
        up = remote(field.at[blk, planes - 1, where], halo.at[0, blk, where], ss, rs.at[k], after)
        down = remote(field.at[blk, 0, where], halo.at[1, blk, where], ss, rs.at[k], before)
        return up, down

    def edge1(slot, i):
        return edge(f0, xh1, x1_s, x1_r, (p, other)[slot], i, rows1(i))

    def edge2(blk, j):
        return edge(f1, xh2, x2_s, x2_r, blk, j, rows2(j))

    def whole(ref, s, r):
        return remote(ref, ref, s, r, mate)

    def lanes(j):
        return pl.ds((j % per) * BLOCK, BLOCK)

    def gradient(field, halo, pln, e, j):
        blk = j // per
        nxt = halo[1, blk, e, :, lanes(j)] if pln == planes - 1 else field[blk, pln + 1, e, :, lanes(j)]
        prv = halo[0, blk, e, :, lanes(j)] if pln == 0 else field[blk, pln - 1, e, :, lanes(j)]
        return nxt, prv

    def slopes(field, halo, de, lo):
        def row(r):
            e = lo + r
            for pln in range(planes):
                nxt, prv = gradient(field, halo, pln, e, 0)
                de[0, pln, e] = nxt - prv
                nxt, prv = gradient(field, halo, pln, e, levels - 1)
                de[1, pln, e] = nxt - prv

        loop(0, ROWS, row)

    def to_below(de, zh, ss, rs, k, where):
        return remote(de.at[0, :, where], zh.at[1, :, where], ss, rs.at[k], below)

    def to_above(de, zh, ss, rs, k, where):
        return remote(de.at[1, :, where], zh.at[0, :, where], ss, rs.at[k], above)

    def z_start(*a):
        @pl.when(has_below)
        def _():
            to_below(*a).start()

        @pl.when(has_above)
        def _():
            to_above(*a).start()

    inner = jnp.logical_and(has_below, has_above)
    outer = jnp.logical_xor(has_below, has_above)

    def z_arrived(de, zh, ss, rs, k, where):
        @pl.when(inner)
        def _():
            whole(zh.at[:, :, where], ss, rs.at[k]).wait_recv()

        @pl.when(outer)
        def _():
            whole(zh.at[0, :, where], ss, rs.at[k]).wait_recv()

    def z_sent(de, ss, where):
        @pl.when(inner)
        def _():
            whole(de.at[:, :, where], ss, ss).wait_send()

        @pl.when(outer)
        def _():
            whole(de.at[0, :, where], ss, ss).wait_send()

    def z1(i):
        return de1, zh1, z1_s, z1_r, i, rows1(i)

    def z2(j):
        return de2, zh2, z2_s, z2_r, j, rows2(j)

    wx = 0.5 * 2.0 * math.sqrt(MA)
    wy = 0.5 * 2.0 * math.sqrt(MB)
    wz = 0.5 * 2.0 * math.sqrt(MC)
    wc = 2.0 * (wx + wy + wz)

    def substep(field, halo, zh, dest, lo):
        def row(r):
            e = lo + r
            for pln in range(planes):
                gas = mask[pln, e]
                pairs = [gradient(field, halo, pln, e, j) for j in range(levels)]
                grads = [zh[0, pln, e]] + [a - b for a, b in pairs] + [zh[1, pln, e]]
                for j in range(levels):
                    blk = j // per
                    mid = field[blk, pln, e, :, lanes(j)]
                    ny = field[blk, pln, e + 1, :, lanes(j)]
                    py = field[blk, pln, e - 1, :, lanes(j)]
                    nz = pltpu.roll(mid, rows_z - 1, 0)
                    pz = pltpu.roll(mid, 1, 0)
                    dy = ny - py
                    dz = nz - pz
                    acc = coef[4 + j : 5 + j, :] * grads[j]
                    acc += coef[4 + levels + j : 5 + levels + j, :] * grads[j + 2]
                    acc += coef[0:1, :] * pltpu.roll(dy, MC, 1)
                    acc += coef[1:2, :] * pltpu.roll(dy, BLOCK - MC, 1)
                    acc += coef[2:3, :] * pltpu.roll(dz, 1, 1)
                    acc += coef[3:4, :] * pltpu.roll(dz, BLOCK - 1, 1)
                    acc += wx * (pairs[j][0] + pairs[j][1]) + wy * (ny + py) + wz * (nz + pz) - wc * mid
                    dest[blk, pln, e, :, lanes(j)] = mid + gas * acc

        loop(0, ROWS, row)

    def slot(j):
        return pl.ds(pl.multiple_of(j * WIDE, WIDE), WIDE)

    def take_low(j):
        total = jnp.zeros((3 * cells, WIDE), jnp.float32)
        for blk in range(2):
            x = tr[blk, :, rows2(j)].reshape(cells, local)
            total += dot(jnp.concatenate(split3(x), axis=0), sel[blk])
        total = total[0:cells] + total[cells : 2 * cells] + total[2 * cells : 3 * cells]
        lx[slot(j), :] = total.T

    def as_source(f):
        for s, (lo, hi) in enumerate(spans):
            pl.when(q == s)(functools.partial(f, s, lo, hi))

    def low_send(j, s, o):
        lo, hi = spans[s]
        return remote(lx.at[pl.ds(pl.multiple_of(j * WIDE + lo, 8), hi - lo)], lr.at[j, s, pl.ds(0, hi - lo)], low_s, meet_r.at[j],
                      (c, o * 2 + p))

    def others(s):
        return [o for o in range(ns) if o != s]

    def collide(j, s, lo, hi):
        lt[...] = lx[slot(j), :]
        for o in others(s):
            first_rank, last_rank = spans[o]
            lt[first_rank:last_rank, :] += lr[j, o, 0 : last_rank - first_rank]
        rt[...] = jnp.zeros_like(rt)

        def step(start, count, columns):
            rows = lt[pl.ds(start, count), :]
            values = lt[0:BASIS_SIZE, :]
            factors = jnp.concatenate(
                [(rows[i : i + 1, :] * values) for i in range(count)], axis=0
            ).astype(jnp.bfloat16)
            rt[lo:hi, :] += dot(table[lo:hi, columns], factors)

        def block(g):
            width = GROUP * BASIS_SIZE
            step(pl.multiple_of(g * GROUP, GROUP), GROUP, pl.ds(pl.multiple_of(g * width, WIDE), width))

        groups = BASIS_SIZE // GROUP
        loop(0, groups, block)
        if groups * GROUP < BASIS_SIZE:
            step(groups * GROUP, BASIS_SIZE - groups * GROUP,
                 pl.ds(groups * GROUP * BASIS_SIZE, (BASIS_SIZE - groups * GROUP) * BASIS_SIZE))

    def lift(j):
        terms = jnp.concatenate(split3(rt[...].T), axis=0)
        for blk in range(2):
            add = dot(terms, sel_t[blk])
            add = (add[0:cells] + add[cells : 2 * cells] + add[2 * cells : 3 * cells]) * DTC
            tr[blk, :, rows2(j)] += add.reshape(planes, ROWS, rows_z, local)

    def give_back(j):
        return remote(tr.at[other, :, rows2(j)], out.at[:, pl.ds(p * half + j * ROWS, ROWS)],
                      back_s, back_r, mate)

    def keep(j):
        return pltpu.make_async_copy(tr.at[p, :, rows2(j)], out.at[:, pl.ds(p * half + j * ROWS, ROWS)],
                                     keep_sem)

    def finish(j):
        give_back(j).start()
        keep(j).start()

    def start_all(copies):
        for copy in copies:
            copy.start()

    def during(index, count, f):
        @pl.when(jnp.logical_and(index >= 0, index < count))
        def _():
            f(index)

    loop(0, 2, lambda k: swap(k).start())
    pltpu.make_async_copy(f0.at[p], f0.at[p], loc_sem).wait()
    loop(0, min(LEAD, first), lambda i: start_all(edge1(0, i)))
    loop(2, arrivals, lambda k: swap(k).start())

    @pl.when(is_source)
    def _():
        raw_copy.start()

    @pl.when(q == 0)
    def _():
        for zh in (zh1, zh2):
            zh[0] = jnp.zeros_like(zh[0])

    @pl.when(q == nq - 1)
    def _():
        for zh in (zh1, zh2):
            zh[1] = jnp.zeros_like(zh[1])

    lane = lax.broadcasted_iota(jnp.int32, (1, BLOCK), 1)
    lane_b, lane_c = lax.div(lane, MC), lax.rem(lane, MC)

    def low_root(x):
        return -0.5 * jnp.sqrt(x.astype(jnp.float32))

    def high_root(x, count):
        return jnp.where(x + 1 < count, -0.5 * jnp.sqrt((x + 1).astype(jnp.float32)), 0.0)

    coef[0:1] = low_root(lane_b)
    coef[1:2] = high_root(lane_b, MB)
    coef[2:3] = low_root(lane_c)
    coef[3:4] = high_root(lane_c, MC)
    wide = lax.broadcasted_iota(jnp.int32, (WIDE, BLOCK), 0)
    for j in range(levels):
        level = q * levels + j
        coef[4 + j : 5 + j] = low_root(0 * lane + level)
        coef[4 + levels + j : 5 + levels + j] = high_root(0 * lane + level, MA)
        mine = jnp.where(rank[pl.ds(level, 1), :] == wide, 1.0, 0.0)
        sel_t[j // per, :, lanes(j)] = mine.astype(jnp.bfloat16)
        sel[j // per, lanes(j), :] = mine.T.astype(jnp.bfloat16)

    clear = [jnp.where(solid[pln] != 0, 0.0, 1.0).astype(jnp.bfloat16) for pln in range(planes)]
    line = lax.broadcasted_iota(jnp.int32, (rows_y, BLOCK), 0)

    def spread(e):
        pick = jnp.where(line == grid_row(p, e), 1.0, 0.0).astype(jnp.bfloat16)
        for pln in range(planes):
            mask[pln, e] = dot(clear[pln], pick) * CFL

    loop(1, ext - 1, spread)

    def advance(t):
        def arrive(i):
            @pl.when(i == 0)
            def _():
                swap_in(0).wait_recv()

            swap_in(i + 1).wait_recv()
            start_all(edge1(1, i))

            @pl.when(i + LEAD < first)
            def _():
                start_all(edge1(0, i + LEAD))

        def slope1(i):
            whole(xh1.at[:, :, rows1(i)], x1_s, x1_r.at[i]).wait_recv()
            slopes(f0, xh1, de1, i * ROWS + 1)
            z_start(*z1(i))

        def slope2(j):
            whole(xh2.at[:, :, rows2(j)], x2_s, x2_r.at[j]).wait_recv()
            slopes(f1, xh2, de2, j * ROWS + 2)
            z_start(*z2(j))

        def move1(i):
            z_arrived(*z1(i))
            substep(f0, xh1, zh1, f1, i * ROWS + 1)

            @pl.when(i >= 1)
            def _():
                for blk in range(2):
                    start_all(edge2(blk, i - 1))

        def move2(j):
            z_arrived(*z2(j))
            substep(f1, xh2, zh2, tr, j * ROWS + 2)

            @pl.when(is_source)
            def _():
                take_low(j)

            as_source(lambda s, lo, hi: start_all(low_send(j, s, o) for o in others(s)))

            @pl.when(jnp.logical_not(is_source))
            def _():
                finish(j)

        def meet(j):
            def one(s, lo, hi):
                if ns > 1:
                    rows = sum(spans[o][1] - spans[o][0] for o in others(s))
                    whole(lx.at[pl.ds(0, rows)], low_s, meet_r.at[j]).wait_recv()
                collide(j, s, lo, hi)
                lift(j)
                finish(j)

            as_source(one)

        during(t, first, arrive)
        during(t - 2, first, slope1)
        during(t - 6, chunks, slope2)
        during(t - 3, first, move1)
        during(t - 7, chunks, move2)

        @pl.when(jnp.logical_and(is_source, t == 8))
        def _():
            raw_copy.wait()

        during(t - 8, chunks, meet)

    loop(0, chunks + 9, advance)

    whole(f0.at[p], swap_s, swap_s).wait_send()
    whole(xh1.at[:, :, pl.ds(1, first * ROWS)], x1_s, x1_s).wait_send()
    whole(xh2.at[:, :, pl.ds(2, half)], x2_s, x2_s).wait_send()
    z_sent(de1, z1_s, pl.ds(1, first * ROWS))
    z_sent(de2, z2_s, pl.ds(2, half))
    if ns > 1:
        as_source(lambda s, lo, hi: whole(
            lr.at[:, pl.ds(0, ns - 1), pl.ds(0, hi - lo)], low_s, low_s).wait_send())

    pltpu.make_async_copy(tr.at[p, :, pl.ds(2, half)], tr.at[p, :, pl.ds(2, half)], keep_sem).wait()
    whole(tr.at[other, :, pl.ds(2, half)], back_s, back_s).wait_send()
    whole(out.at[:, pl.ds(other * half, half)], back_r, back_r).wait_recv()


def body(hermite_coefficient_array, encounter_kernel_array, obstacle_indicator):
    planes, rows_y, rows_z, local = hermite_coefficient_array.shape
    nc = lax.axis_size("cells")
    nm = lax.axis_size("modes")
    per = local // BLOCK
    levels = 2 * per
    half = rows_y // 2
    ns = -(-(LDEG + 1) // levels)
    chunks = half // ROWS
    ext = half + 4

    index = np.arange(MODES)
    flags = (index // BLOCK + index // MC % MB + index % MC <= LDEG).astype(np.int32)
    rank = jnp.asarray(np.where(flags == 1, np.cumsum(flags) - 1, -1).reshape(MA, BLOCK), jnp.int32)

    marks = [int(flags[: min(s * levels, MA) * BLOCK].sum()) for s in range(ns + 1)]
    spans = [(lo // 16 * 16, min(-(-hi // 16) * 16, BASIS_SIZE)) for lo, hi in zip(marks[:-1], marks[1:])]
    cells = planes * ROWS * rows_z
    field = pltpu.VMEM((2, planes, ext, rows_z, local), jnp.float32)
    halo = pltpu.VMEM((2, 2, ext, rows_z, local), jnp.float32)
    slope = pltpu.VMEM((2, planes, ext, rows_z, BLOCK), jnp.float32)
    dma = pltpu.SemaphoreType.DMA
    cfg = (planes, rows_y, rows_z, local, nc, nm, spans)
    vmem = pl.BlockSpec(memory_space=pltpu.VMEM)
    anywhere = pl.BlockSpec(memory_space=pl.ANY)
    return pl.pallas_call(
        functools.partial(kernel, cfg),
        out_shape=pltpu.VMEM(hermite_coefficient_array.shape, jnp.float32),
        in_specs=[anywhere, vmem, vmem, anywhere],
        out_specs=vmem,
        scratch_shapes=[
            field, field, field, halo, halo, slope, slope, slope, slope,
            pltpu.VMEM((planes, ext, rows_z, BLOCK), jnp.float32),
            pltpu.VMEM((4 + 2 * levels + -(4 + 2 * levels) % 8, BLOCK), jnp.float32),
            pltpu.VMEM((2, local, WIDE), jnp.bfloat16),
            pltpu.VMEM((2, WIDE, local), jnp.bfloat16),
            pltpu.VMEM((chunks * WIDE, cells), jnp.float32),
            pltpu.VMEM((chunks, ns, max(hi - lo for lo, hi in spans), cells), jnp.float32),
            pltpu.VMEM((BASIS_SIZE, BASIS_SIZE * BASIS_SIZE), jnp.bfloat16),
            pltpu.VMEM((WIDE, cells), jnp.float32),
            pltpu.VMEM((WIDE, cells), jnp.float32),
            dma, dma, dma, dma((ext // ROWS,)), dma, dma((chunks + 1,)), dma, dma((chunks,)),
            dma, dma((chunks + 1,)), dma, dma((chunks,)), dma, dma((chunks,)), dma, dma, dma,
        ],
        compiler_params=pltpu.CompilerParams(
            collective_id=0, has_side_effects=True, vmem_limit_bytes=54 * 1024 * 1024
        ),
    )(hermite_coefficient_array, obstacle_indicator.transpose(0, 2, 1), rank, encounter_kernel_array.T)


def solution(mesh):
    placed = (P("cells", None, None, "modes"), P(), P("cells", None, None))
    return jax.shard_map(
        body, mesh=mesh, in_specs=placed, out_specs=P("cells", None, None, "modes"), check_vma=False
    )
```

```python
import functools
import math

import jax
import jax.numpy as jnp
import numpy as np
from jax import lax
from jax.experimental import pallas as pl
from jax.experimental.pallas import tpu as pltpu
from jax.sharding import PartitionSpec as P

MA = 16
MB = 16
MC = 8
LDEG = 7
BASIS_SIZE = 120
MODES = 2048
BLOCK = MB * MC
WIDE = 128
GROUP = 64
ROWS = 2
LEAD = 8
EARLY = 6

CFL = 0.04
DTC = 0.2
MESH = pl.DeviceIdType.MESH


def split3(x):
    hi = x.astype(jnp.bfloat16)
    rest = x - hi.astype(jnp.float32)
    mid = rest.astype(jnp.bfloat16)
    low = (rest - mid.astype(jnp.float32)).astype(jnp.bfloat16)
    return hi, mid, low


def dot(a, b):
    return jnp.dot(a, b, preferred_element_type=jnp.float32)


def loop(lo, hi, f):
    def step(i, carry):
        f(i)
        return carry

    lax.fori_loop(lo, hi, step, 0)


def kernel(cfg, hin, solid, rank, raw, out, f0, f1, tr, xh1, xh2, zh1, zh2, de1, de2,
           mask, coef, sel, sel_t, lx, lr, table, lt, rt, raw_sem, loc_sem, swap_s, swap_r,
           x1_s, x1_r, x2_s, x2_r, x3_r, z1_s, z1_r, z2_s, z2_r, low_s, meet_r, brink_s, brink_r, back_s, back_r, keep_sem):
    planes, rows_y, rows_z, local, nc, nm, spans = cfg
    ns = len(spans)
    per = local // BLOCK
    levels = 2 * per
    half = rows_y // 2
    ext = half + 4
    nq = nm // 2
    chunks = half // ROWS
    cells = planes * ROWS * rows_z

    c = lax.axis_index("cells")
    m = lax.axis_index("modes")
    p = lax.rem(m, 2)
    q = lax.div(m, 2)
    other = 1 - p
    mate = (c, q * 2 + other)
    before = (lax.rem(c + nc - 1, nc), m)
    after = (lax.rem(c + 1, nc), m)
    below = (c, m - 2)
    above = (c, m + 2)
    has_below = q > 0
    has_above = q < nq - 1
    is_source = q < ns

    def peer(d):
        return (c, lax.rem(q + d, ns) * 2 + p)

    barrier = pltpu.get_barrier_semaphore()

    def greet(dev):
        pl.semaphore_signal(barrier, inc=1, device_id=dev, device_id_type=MESH)

    for dev in (mate, before, after):
        greet(dev)

    @pl.when(has_below)
    def _():
        greet(below)

    @pl.when(has_above)
    def _():
        greet(above)

    @pl.when(is_source)
    def _():
        for d in range(1, ns):
            greet(peer(d))

    def grid_row(side, e):
        return lax.rem(side * half + (rows_y - 2) + e, rows_y)

    own_pieces = [(1, 2), (2, half + 2), (half + 2, half + 3)]

    def own(i):
        lo, hi = own_pieces[i]
        return pltpu.make_async_copy(
            hin.at[:, pl.ds(grid_row(p, lo), hi - lo)],
            f0.at[p, :, pl.ds(lo, hi - lo)],
            loc_sem,
        )

    for i in range(len(own_pieces)):
        own(i).start()
    raw_copy = pltpu.make_async_copy(raw, table, raw_sem)

    greeted = 3 + has_below.astype(jnp.int32) + has_above.astype(jnp.int32)
    pl.semaphore_wait(barrier, greeted + (ns - 1) * is_source.astype(jnp.int32))

    def remote(src, dst, s, r, dev):
        return pltpu.make_async_remote_copy(
            src_ref=src, dst_ref=dst, send_sem=s, recv_sem=r, device_id=dev, device_id_type=MESH
        )

    brinks = (1, half + 2)

    def pair(u):
        return pl.ds(u * ROWS + 2, ROWS)

    def turn(i):
        return lax.rem(i + chunks - 1, chunks)

    def late(k):
        return k + lax.div(k, chunks - 2) * (2 * chunks - 3 - 2 * k)

    def swap(u, who):
        return remote(hin.at[:, pl.ds(grid_row(other, u * ROWS + 2), ROWS)], f0.at[who, :, pair(u)],
                      swap_s, swap_r.at[u], mate)

    def swap_brink(n, who):
        return remote(hin.at[:, pl.ds(grid_row(other, brinks[n]), 1)], f0.at[who, :, pl.ds(brinks[n], 1)],
                      swap_s, swap_r.at[chunks + n], mate)

    def brink(n):
        return remote(f1.at[:, :, pl.ds((half + 1, 2)[n], 1)], f1.at[:, :, pl.ds(brinks[n], 1)],
                      brink_s, brink_r.at[n], mate)

    def edge(field, halo, ss, rs, blk, k, where, span):
        up = remote(field.at[blk, planes - 1, where, :, span], halo.at[0, blk, where, :, span], ss, rs.at[k], after)
        down = remote(field.at[blk, 0, where, :, span], halo.at[1, blk, where, :, span], ss, rs.at[k], before)
        return up, down

    def edge1(blk, u):
        return edge(f0, xh1, x1_s, x1_r, blk, u, pair(u), pl.ds(0, local))

    def edge2(blk, u):
        return edge(f1, xh2, x2_s, x2_r, blk, u, pair(u), pl.ds((local - BLOCK) * blk, BLOCK))

    def edge3(blk, u):
        return edge(f1, xh2, x2_s, x3_r, blk, u, pair(u), pl.ds(BLOCK * (1 - blk), local - BLOCK))

    def whole(ref, s, r):
        return remote(ref, ref, s, r, mate)

    def lanes(j):
        return pl.ds((j % per) * BLOCK, BLOCK)

    def gradient(field, halo, pln, e, j):
        blk = j // per
        nxt = halo[1, blk, e, :, lanes(j)] if pln == planes - 1 else field[blk, pln + 1, e, :, lanes(j)]
        prv = halo[0, blk, e, :, lanes(j)] if pln == 0 else field[blk, pln - 1, e, :, lanes(j)]
        return nxt, prv

    def slopes(field, halo, de, lo):
        def row(r):
            e = lo + r
            for pln in range(planes):
                nxt, prv = gradient(field, halo, pln, e, 0)
                de[0, pln, e] = nxt - prv
                nxt, prv = gradient(field, halo, pln, e, levels - 1)
                de[1, pln, e] = nxt - prv

        loop(0, ROWS, row)

    def to_below(de, zh, ss, rs, k, where):
        return remote(de.at[0, :, where], zh.at[1, :, where], ss, rs.at[k], below)

    def to_above(de, zh, ss, rs, k, where):
        return remote(de.at[1, :, where], zh.at[0, :, where], ss, rs.at[k], above)

    def z_start(*a):
        @pl.when(has_below)
        def _():
            to_below(*a).start()

        @pl.when(has_above)
        def _():
            to_above(*a).start()

    inner = jnp.logical_and(has_below, has_above)
    outer = jnp.logical_xor(has_below, has_above)

    def z_arrived(de, zh, ss, rs, k, where):
        @pl.when(inner)
        def _():
            whole(zh.at[:, :, where], ss, rs.at[k]).wait_recv()

        @pl.when(outer)
        def _():
            whole(zh.at[0, :, where], ss, rs.at[k]).wait_recv()

    def z_sent(de, ss, where):
        @pl.when(inner)
        def _():
            whole(de.at[:, :, where], ss, ss).wait_send()

        @pl.when(outer)
        def _():
            whole(de.at[0, :, where], ss, ss).wait_send()

    def z1(u):
        return de1, zh1, z1_s, z1_r, u, pair(u)

    def z2(u):
        return de2, zh2, z2_s, z2_r, u, pair(u)

    wx = 0.5 * 2.0 * math.sqrt(MA)
    wy = 0.5 * 2.0 * math.sqrt(MB)
    wz = 0.5 * 2.0 * math.sqrt(MC)
    wc = 2.0 * (wx + wy + wz)

    def substep(field, halo, zh, dest, lo):
        def row(r):
            e = lo + r
            for pln in range(planes):
                gas = mask[pln, e]
                pairs = [gradient(field, halo, pln, e, j) for j in range(levels)]
                grads = [zh[0, pln, e]] + [a - b for a, b in pairs] + [zh[1, pln, e]]
                for j in range(levels):
                    blk = j // per
                    mid = field[blk, pln, e, :, lanes(j)]
                    ny = field[blk, pln, e + 1, :, lanes(j)]
                    py = field[blk, pln, e - 1, :, lanes(j)]
                    nz = pltpu.roll(mid, rows_z - 1, 0)
                    pz = pltpu.roll(mid, 1, 0)
                    dy = ny - py
                    dz = nz - pz
                    acc = coef[4 + j : 5 + j, :] * grads[j]
                    acc += coef[4 + levels + j : 5 + levels + j, :] * grads[j + 2]
                    acc += coef[0:1, :] * pltpu.roll(dy, MC, 1)
                    acc += coef[1:2, :] * pltpu.roll(dy, BLOCK - MC, 1)
                    acc += coef[2:3, :] * pltpu.roll(dz, 1, 1)
                    acc += coef[3:4, :] * pltpu.roll(dz, BLOCK - 1, 1)
                    acc += wx * (pairs[j][0] + pairs[j][1]) + wy * (ny + py) + wz * (nz + pz) - wc * mid
                    dest[blk, pln, e, :, lanes(j)] = mid + gas * acc

        loop(0, ROWS, row)

    def slot(j):
        return pl.ds(pl.multiple_of(j * WIDE, WIDE), WIDE)

    def take_low(j):
        total = jnp.zeros((3 * cells, WIDE), jnp.float32)
        for blk in range(2):
            x = tr[blk, :, pair(j)].reshape(cells, local)
            total += dot(jnp.concatenate(split3(x), axis=0), sel[blk])
        total = total[0:cells] + total[cells : 2 * cells] + total[2 * cells : 3 * cells]
        lx[slot(j), :] = total.T

    def as_source(f):
        for s, (lo, hi) in enumerate(spans):
            pl.when(q == s)(functools.partial(f, s, lo, hi))

    def low_send(j, s, o):
        lo, hi = spans[s]
        return remote(lx.at[pl.ds(pl.multiple_of(j * WIDE + lo, 8), hi - lo)], lr.at[j, s, pl.ds(0, hi - lo)], low_s, meet_r.at[j],
                      (c, o * 2 + p))

    def others(s):
        return [o for o in range(ns) if o != s]

    def collide(j, s, lo, hi):
        lt[...] = lx[slot(j), :]
        for o in others(s):
            first_rank, last_rank = spans[o]
            lt[first_rank:last_rank, :] += lr[j, o, 0 : last_rank - first_rank]
        rt[...] = jnp.zeros_like(rt)

        def step(start, count, columns):
            rows = lt[pl.ds(start, count), :]
            values = lt[0:BASIS_SIZE, :]
            factors = jnp.concatenate(
                [(rows[i : i + 1, :] * values) for i in range(count)], axis=0
            ).astype(jnp.bfloat16)
            rt[lo:hi, :] += dot(table[lo:hi, columns], factors)

        def block(g):
            width = GROUP * BASIS_SIZE
            step(pl.multiple_of(g * GROUP, GROUP), GROUP, pl.ds(pl.multiple_of(g * width, WIDE), width))

        groups = BASIS_SIZE // GROUP
        loop(0, groups, block)
        if groups * GROUP < BASIS_SIZE:
            step(groups * GROUP, BASIS_SIZE - groups * GROUP,
                 pl.ds(groups * GROUP * BASIS_SIZE, (BASIS_SIZE - groups * GROUP) * BASIS_SIZE))

    def lift(j):
        terms = jnp.concatenate(split3(rt[...].T), axis=0)
        for blk in range(2):
            add = dot(terms, sel_t[blk])
            add = (add[0:cells] + add[cells : 2 * cells] + add[2 * cells : 3 * cells]) * DTC
            tr[blk, :, pair(j)] += add.reshape(planes, ROWS, rows_z, local)

    def give_back(j):
        return remote(tr.at[other, :, pair(j)], out.at[:, pl.ds(p * half + j * ROWS, ROWS)],
                      back_s, back_r, mate)

    def keep(j):
        return pltpu.make_async_copy(tr.at[p, :, pair(j)], out.at[:, pl.ds(p * half + j * ROWS, ROWS)],
                                     keep_sem)

    def finish(j):
        give_back(j).start()
        keep(j).start()

    def start_all(copies):
        for copy in copies:
            copy.start()

    def during(index, count, f):
        @pl.when(jnp.logical_and(index >= 0, index < count))
        def _():
            f(index)

    swap(chunks - 1, p).start()
    near = pl.ds(1, half + 2)
    pltpu.make_async_copy(f0.at[p, :, near], f0.at[p, :, near], loc_sem).wait()
    loop(0, min(LEAD, chunks), lambda i: start_all(edge1(p, turn(i))))
    swap(chunks - 2, p).start()
    for n in (1, 0):
        swap_brink(n, p).start()
    early = min(EARLY, chunks - 2)
    loop(0, early, lambda u: swap(u, p).start())

    @pl.when(is_source)
    def _():
        raw_copy.start()

    @pl.when(q == 0)
    def _():
        for zh in (zh1, zh2):
            zh[0] = jnp.zeros_like(zh[0])

    @pl.when(q == nq - 1)
    def _():
        for zh in (zh1, zh2):
            zh[1] = jnp.zeros_like(zh[1])

    lane = lax.broadcasted_iota(jnp.int32, (1, BLOCK), 1)
    lane_b, lane_c = lax.div(lane, MC), lax.rem(lane, MC)

    def low_root(x):
        return -0.5 * jnp.sqrt(x.astype(jnp.float32))

    def high_root(x, count):
        return jnp.where(x + 1 < count, -0.5 * jnp.sqrt((x + 1).astype(jnp.float32)), 0.0)

    coef[0:1] = low_root(lane_b)
    coef[1:2] = high_root(lane_b, MB)
    coef[2:3] = low_root(lane_c)
    coef[3:4] = high_root(lane_c, MC)
    wide = lax.broadcasted_iota(jnp.int32, (WIDE, BLOCK), 0)
    for j in range(levels):
        level = q * levels + j
        coef[4 + j : 5 + j] = low_root(0 * lane + level)
        coef[4 + levels + j : 5 + levels + j] = high_root(0 * lane + level, MA)
        mine = jnp.where(rank[pl.ds(level, 1), :] == wide, 1.0, 0.0)
        sel_t[j // per, :, lanes(j)] = mine.astype(jnp.bfloat16)
        sel[j // per, lanes(j), :] = mine.T.astype(jnp.bfloat16)

    clear = [jnp.where(solid[pln] != 0, 0.0, 1.0).astype(jnp.bfloat16) for pln in range(planes)]
    line = lax.broadcasted_iota(jnp.int32, (rows_y, BLOCK), 0)

    def spread(e):
        pick = jnp.where(line == grid_row(p, e), 1.0, 0.0).astype(jnp.bfloat16)
        for pln in range(planes):
            mask[pln, e] = dot(clear[pln], pick) * CFL

    loop(2, half + 2, spread)

    def advance(t):
        def arrive(i):
            u = turn(i)

            @pl.when(i == 1)
            def _():
                swap(chunks - 2, other).wait_recv()
                for n in (1, 0):
                    swap_brink(n, other).wait_recv()

            @pl.when(i < chunks - 1)
            def _():
                swap(u, other).wait_recv()

            start_all(edge1(other, u))

            @pl.when(i + LEAD < chunks)
            def _():
                start_all(edge1(p, turn(i + LEAD)))

        def slope1(i):
            u = turn(i)
            whole(xh1.at[:, :, pair(u)], x1_s, x1_r.at[u]).wait_recv()
            slopes(f0, xh1, de1, u * ROWS + 2)
            z_start(*z1(u))

        def slope2(k):
            u = late(k)
            whole(xh2.at[:, :, pair(u), :, pl.ds(0, BLOCK)], x2_s, x2_r.at[u]).wait_recv()
            slopes(f1, xh2, de2, u * ROWS + 2)
            z_start(*z2(u))

        def move1(i):
            u = turn(i)
            z_arrived(*z1(u))
            substep(f0, xh1, zh1, f1, u * ROWS + 2)
            for n in range(2):
                @pl.when(i == n)
                def _(n=n):
                    brink(n).start()
                    if n == 1:
                        loop(early, chunks - 2, lambda u: swap(u, p).start())

            for blk in range(2):
                start_all(edge2(blk, u))
            if per > 1:
                for blk in range(2):
                    start_all(edge3(blk, u))

        def move2(k):
            u = late(k)
            for n, turn_of in enumerate((0, chunks - 2)):
                @pl.when(k == turn_of)
                def _(n=n):
                    brink(n).wait_recv()

            if per > 1:
                whole(xh2.at[:, :, pair(u), :, pl.ds(BLOCK, local - BLOCK)], x2_s, x3_r.at[u]).wait_recv()
            z_arrived(*z2(u))
            substep(f1, xh2, zh2, tr, u * ROWS + 2)

            @pl.when(is_source)
            def _():
                take_low(u)

            as_source(lambda s, lo, hi: start_all(low_send(u, s, o) for o in others(s)))

            @pl.when(jnp.logical_not(is_source))
            def _():
                finish(u)

        def meet(k):
            j = late(k)

            def one(s, lo, hi):
                if ns > 1:
                    rows = sum(spans[o][1] - spans[o][0] for o in others(s))
                    whole(lx.at[pl.ds(0, rows)], low_s, meet_r.at[j]).wait_recv()
                collide(j, s, lo, hi)
                lift(j)
                finish(j)

            as_source(one)

        during(t, chunks, arrive)
        during(t - 1, chunks, slope1)
        during(t - 2, chunks, move1)
        during(t - 4, chunks, slope2)
        during(t - 5, chunks, move2)
        @pl.when(jnp.logical_and(is_source, t == 6))
        def _():
            raw_copy.wait()

        during(t - 6, chunks, meet)

    loop(0, chunks + 6, advance)

    whole(f0.at[p, :, near], swap_s, swap_s).wait_send()
    whole(xh1.at[:, :, pl.ds(2, half)], x1_s, x1_s).wait_send()
    whole(f1.at[:, :, pl.ds(2, 2)], brink_s, brink_s).wait_send()
    whole(xh2.at[:, :, pl.ds(2, half)], x2_s, x2_s).wait_send()
    z_sent(de1, z1_s, pl.ds(2, half))
    z_sent(de2, z2_s, pl.ds(2, half))
    if ns > 1:
        as_source(lambda s, lo, hi: whole(
            lr.at[:, pl.ds(0, ns - 1), pl.ds(0, hi - lo)], low_s, low_s).wait_send())

    pltpu.make_async_copy(tr.at[p, :, pl.ds(2, half)], tr.at[p, :, pl.ds(2, half)], keep_sem).wait()
    whole(tr.at[other, :, pl.ds(2, half)], back_s, back_s).wait_send()
    whole(out.at[:, pl.ds(other * half, half)], back_r, back_r).wait_recv()


def body(hermite_coefficient_array, encounter_kernel_array, obstacle_indicator):
    planes, rows_y, rows_z, local = hermite_coefficient_array.shape
    nc = lax.axis_size("cells")
    nm = lax.axis_size("modes")
    per = local // BLOCK
    levels = 2 * per
    half = rows_y // 2
    ns = -(-(LDEG + 1) // levels)
    chunks = half // ROWS
    ext = half + 4

    index = np.arange(MODES)
    flags = (index // BLOCK + index // MC % MB + index % MC <= LDEG).astype(np.int32)
    rank = jnp.asarray(np.where(flags == 1, np.cumsum(flags) - 1, -1).reshape(MA, BLOCK), jnp.int32)

    marks = [int(flags[: min(s * levels, MA) * BLOCK].sum()) for s in range(ns + 1)]
    spans = [(lo // 16 * 16, min(-(-hi // 16) * 16, BASIS_SIZE)) for lo, hi in zip(marks[:-1], marks[1:])]
    cells = planes * ROWS * rows_z
    field = pltpu.VMEM((2, planes, ext, rows_z, local), jnp.float32)
    halo = pltpu.VMEM((2, 2, ext, rows_z, local), jnp.float32)
    slope = pltpu.VMEM((2, planes, ext, rows_z, BLOCK), jnp.float32)
    dma = pltpu.SemaphoreType.DMA
    cfg = (planes, rows_y, rows_z, local, nc, nm, spans)
    vmem = pl.BlockSpec(memory_space=pltpu.VMEM)
    anywhere = pl.BlockSpec(memory_space=pl.ANY)
    return pl.pallas_call(
        functools.partial(kernel, cfg),
        out_shape=pltpu.VMEM(hermite_coefficient_array.shape, jnp.float32),
        in_specs=[anywhere, vmem, vmem, anywhere],
        out_specs=vmem,
        scratch_shapes=[
            field, field, field, halo, halo, slope, slope, slope, slope,
            pltpu.VMEM((planes, ext, rows_z, BLOCK), jnp.float32),
            pltpu.VMEM((4 + 2 * levels + -(4 + 2 * levels) % 8, BLOCK), jnp.float32),
            pltpu.VMEM((2, local, WIDE), jnp.bfloat16),
            pltpu.VMEM((2, WIDE, local), jnp.bfloat16),
            pltpu.VMEM((chunks * WIDE, cells), jnp.float32),
            pltpu.VMEM((chunks, ns, max(hi - lo for lo, hi in spans), cells), jnp.float32),
            pltpu.VMEM((BASIS_SIZE, BASIS_SIZE * BASIS_SIZE), jnp.bfloat16),
            pltpu.VMEM((WIDE, cells), jnp.float32),
            pltpu.VMEM((WIDE, cells), jnp.float32),
            dma, dma, dma, dma((chunks + 2,)), dma, dma((chunks,)), dma, dma((chunks,)), dma((chunks,)),
            dma, dma((chunks,)), dma, dma((chunks,)), dma, dma((chunks,)), dma, dma((2,)), dma, dma, dma,
        ],
        compiler_params=pltpu.CompilerParams(
            collective_id=0, has_side_effects=True, vmem_limit_bytes=54 * 1024 * 1024
        ),
    )(hermite_coefficient_array, obstacle_indicator.transpose(0, 2, 1), rank, encounter_kernel_array.T)


def solution(mesh):
    placed = (P("cells", None, None, "modes"), P(), P("cells", None, None))
    return jax.shard_map(
        body, mesh=mesh, in_specs=placed, out_specs=P("cells", None, None, "modes"), check_vma=False
    )
```

```python
import functools
import math

import jax
import jax.numpy as jnp
import numpy as np
from jax import lax
from jax.experimental import pallas as pl
from jax.experimental.pallas import tpu as pltpu
from jax.sharding import PartitionSpec as P

MA = 16
MB = 16
MC = 8
LDEG = 7
BASIS_SIZE = 120
MODES = 2048
BLOCK = MB * MC
WIDE = 128
GROUP = 64
ROWS = 2
LEAD = 8
RING = 8
EARLY = 6

CFL = 0.04
DTC = 0.2
MESH = pl.DeviceIdType.MESH


def split3(x):
    hi = x.astype(jnp.bfloat16)
    rest = x - hi.astype(jnp.float32)
    mid = rest.astype(jnp.bfloat16)
    low = (rest - mid.astype(jnp.float32)).astype(jnp.bfloat16)
    return hi, mid, low


def dot(a, b):
    return jnp.dot(a, b, preferred_element_type=jnp.float32)


def loop(lo, hi, f):
    def step(i, carry):
        f(i)
        return carry

    lax.fori_loop(lo, hi, step, 0)


def kernel(cfg, hin, solid, rank, raw, out, f0, f1, tr, xh1, xh2, zh1, zh2, de1, de2,
           mask, coef, sel, sel_t, lx, lr, table, lt, rt, raw_sem, loc_sem, swap_s, swap_r,
           x1_s, x1_r, x2_s, x2_r, x3_r, z1_s, z1_r, z2_s, z2_r, low_s, meet_r, brink_s, brink_r, back_s, back_r, keep_sem):
    planes, rows_y, rows_z, local, nc, nm, spans = cfg
    ns = len(spans)
    per = local // BLOCK
    levels = 2 * per
    half = rows_y // 2
    ext = half + 4
    nq = nm // 2
    chunks = half // ROWS
    cells = planes * ROWS * rows_z

    c = lax.axis_index("cells")
    m = lax.axis_index("modes")
    p = lax.rem(m, 2)
    q = lax.div(m, 2)
    other = 1 - p
    mate = (c, q * 2 + other)
    before = (lax.rem(c + nc - 1, nc), m)
    after = (lax.rem(c + 1, nc), m)
    below = (c, m - 2)
    above = (c, m + 2)
    has_below = q > 0
    has_above = q < nq - 1
    is_source = q < ns

    def peer(d):
        return (c, lax.rem(q + d, ns) * 2 + p)

    barrier = pltpu.get_barrier_semaphore()

    def greet(dev):
        pl.semaphore_signal(barrier, inc=1, device_id=dev, device_id_type=MESH)

    for dev in (mate, before, after):
        greet(dev)

    @pl.when(has_below)
    def _():
        greet(below)

    @pl.when(has_above)
    def _():
        greet(above)

    @pl.when(is_source)
    def _():
        for d in range(1, ns):
            greet(peer(d))

    def grid_row(side, e):
        return lax.rem(side * half + (rows_y - 2) + e, rows_y)

    own_pieces = [(1, 2), (2, half + 2), (half + 2, half + 3)]

    def own(i):
        lo, hi = own_pieces[i]
        return pltpu.make_async_copy(
            hin.at[:, pl.ds(grid_row(p, lo), hi - lo)],
            f0.at[p, :, pl.ds(lo, hi - lo)],
            loc_sem,
        )

    for i in range(len(own_pieces)):
        own(i).start()
    raw_copy = pltpu.make_async_copy(raw, table, raw_sem)

    greeted = 3 + has_below.astype(jnp.int32) + has_above.astype(jnp.int32)
    pl.semaphore_wait(barrier, greeted + (ns - 1) * is_source.astype(jnp.int32))

    def remote(src, dst, s, r, dev):
        return pltpu.make_async_remote_copy(
            src_ref=src, dst_ref=dst, send_sem=s, recv_sem=r, device_id=dev, device_id_type=MESH
        )

    brinks = (1, half + 2)

    def pair(u):
        return pl.ds(u * ROWS + 2, ROWS)

    def turn(i):
        return lax.rem(i + chunks - 1, chunks)

    def late(k):
        return k + lax.div(k, chunks - 2) * (2 * chunks - 3 - 2 * k)

    def ring(u):
        return lax.rem(u, RING)

    def ring2(u):
        return lax.rem(u, RING) + lax.div(u, chunks - 1) * (RING - (chunks - 1) % RING)

    def swap(u, who):
        return remote(hin.at[:, pl.ds(grid_row(other, u * ROWS + 2), ROWS)], f0.at[who, :, pair(u)],
                      swap_s, swap_r.at[u], mate)

    def swap_brink(n, who):
        return remote(hin.at[:, pl.ds(grid_row(other, brinks[n]), 1)], f0.at[who, :, pl.ds(brinks[n], 1)],
                      swap_s, swap_r.at[chunks + n], mate)

    def brink(n):
        return remote(f1.at[:, :, pl.ds((half + 1, 2)[n], 1)], f1.at[:, :, pl.ds(brinks[n], 1)],
                      brink_s, brink_r.at[n], mate)

    def edge(field, halo, ss, rs, blk, k, where, span):
        up = remote(field.at[blk, planes - 1, where, :, span], halo.at[0, blk, where, :, span], ss, rs.at[k], after)
        down = remote(field.at[blk, 0, where, :, span], halo.at[1, blk, where, :, span], ss, rs.at[k], before)
        return up, down

    def edge1(blk, u):
        return edge(f0, xh1, x1_s, x1_r, blk, u, pair(u), pl.ds(0, local))

    def edge2(blk, u):
        return edge(f1, xh2, x2_s, x2_r, blk, ring2(u), pair(u), pl.ds((local - BLOCK) * blk, BLOCK))

    def edge3(blk, u):
        return edge(f1, xh2, x2_s, x3_r, blk, ring2(u), pair(u), pl.ds(BLOCK * (1 - blk), local - BLOCK))

    def whole(ref, s, r):
        return remote(ref, ref, s, r, mate)

    def lanes(j):
        return pl.ds((j % per) * BLOCK, BLOCK)

    def gradient(field, halo, pln, e, j):
        blk = j // per
        nxt = halo[1, blk, e, :, lanes(j)] if pln == planes - 1 else field[blk, pln + 1, e, :, lanes(j)]
        prv = halo[0, blk, e, :, lanes(j)] if pln == 0 else field[blk, pln - 1, e, :, lanes(j)]
        return nxt, prv

    def slopes(field, halo, de, lo):
        def row(r):
            e = lo + r
            for pln in range(planes):
                nxt, prv = gradient(field, halo, pln, e, 0)
                de[0, pln, e] = nxt - prv
                nxt, prv = gradient(field, halo, pln, e, levels - 1)
                de[1, pln, e] = nxt - prv

        loop(0, ROWS, row)

    def to_below(de, zh, ss, rs, k, where):
        return remote(de.at[0, :, where], zh.at[1, :, where], ss, rs.at[k], below)

    def to_above(de, zh, ss, rs, k, where):
        return remote(de.at[1, :, where], zh.at[0, :, where], ss, rs.at[k], above)

    def z_start(*a):
        @pl.when(has_below)
        def _():
            to_below(*a).start()

        @pl.when(has_above)
        def _():
            to_above(*a).start()

    inner = jnp.logical_and(has_below, has_above)
    outer = jnp.logical_xor(has_below, has_above)

    def z_arrived(de, zh, ss, rs, k, where):
        @pl.when(inner)
        def _():
            whole(zh.at[:, :, where], ss, rs.at[k]).wait_recv()

        @pl.when(outer)
        def _():
            whole(zh.at[0, :, where], ss, rs.at[k]).wait_recv()

    def z_sent(de, ss, where):
        @pl.when(inner)
        def _():
            whole(de.at[:, :, where], ss, ss).wait_send()

        @pl.when(outer)
        def _():
            whole(de.at[0, :, where], ss, ss).wait_send()

    def z1(u):
        return de1, zh1, z1_s, z1_r, ring(u), pair(u)

    def z2(u):
        return de2, zh2, z2_s, z2_r, ring(u), pair(u)

    wx = 0.5 * 2.0 * math.sqrt(MA)
    wy = 0.5 * 2.0 * math.sqrt(MB)
    wz = 0.5 * 2.0 * math.sqrt(MC)
    wc = 2.0 * (wx + wy + wz)

    def substep(field, halo, zh, dest, lo):
        def row(r):
            e = lo + r
            for pln in range(planes):
                gas = mask[pln, e]
                pairs = [gradient(field, halo, pln, e, j) for j in range(levels)]
                grads = [zh[0, pln, e]] + [a - b for a, b in pairs] + [zh[1, pln, e]]
                for j in range(levels):
                    blk = j // per
                    mid = field[blk, pln, e, :, lanes(j)]
                    ny = field[blk, pln, e + 1, :, lanes(j)]
                    py = field[blk, pln, e - 1, :, lanes(j)]
                    nz = pltpu.roll(mid, rows_z - 1, 0)
                    pz = pltpu.roll(mid, 1, 0)
                    dy = ny - py
                    dz = nz - pz
                    acc = coef[4 + j : 5 + j, :] * grads[j]
                    acc += coef[4 + levels + j : 5 + levels + j, :] * grads[j + 2]
                    acc += coef[0:1, :] * pltpu.roll(dy, MC, 1)
                    acc += coef[1:2, :] * pltpu.roll(dy, BLOCK - MC, 1)
                    acc += coef[2:3, :] * pltpu.roll(dz, 1, 1)
                    acc += coef[3:4, :] * pltpu.roll(dz, BLOCK - 1, 1)
                    acc += wx * (pairs[j][0] + pairs[j][1]) + wy * (ny + py) + wz * (nz + pz) - wc * mid
                    dest[blk, pln, e, :, lanes(j)] = mid + gas * acc

        loop(0, ROWS, row)

    def slot(j):
        return pl.ds(pl.multiple_of(j * WIDE, WIDE), WIDE)

    def take_low(j):
        total = jnp.zeros((3 * cells, WIDE), jnp.float32)
        for blk in range(2):
            x = tr[blk, :, pair(j)].reshape(cells, local)
            total += dot(jnp.concatenate(split3(x), axis=0), sel[blk])
        total = total[0:cells] + total[cells : 2 * cells] + total[2 * cells : 3 * cells]
        lx[slot(j), :] = total.T

    def as_source(f):
        for s, (lo, hi) in enumerate(spans):
            pl.when(q == s)(functools.partial(f, s, lo, hi))

    def low_send(j, s, o):
        lo, hi = spans[s]
        return remote(lx.at[pl.ds(pl.multiple_of(j * WIDE + lo, 8), hi - lo)], lr.at[j, s, pl.ds(0, hi - lo)], low_s, meet_r.at[ring(j)],
                      (c, o * 2 + p))

    def others(s):
        return [o for o in range(ns) if o != s]

    def collide(j, s, lo, hi):
        lt[...] = lx[slot(j), :]
        for o in others(s):
            first_rank, last_rank = spans[o]
            lt[first_rank:last_rank, :] += lr[j, o, 0 : last_rank - first_rank]
        rt[...] = jnp.zeros_like(rt)

        def step(start, count, columns):
            rows = lt[pl.ds(start, count), :]
            values = lt[0:BASIS_SIZE, :]
            factors = jnp.concatenate(
                [(rows[i : i + 1, :] * values) for i in range(count)], axis=0
            ).astype(jnp.bfloat16)
            rt[lo:hi, :] += dot(table[lo:hi, columns], factors)

        def block(g):
            width = GROUP * BASIS_SIZE
            step(pl.multiple_of(g * GROUP, GROUP), GROUP, pl.ds(pl.multiple_of(g * width, WIDE), width))

        groups = BASIS_SIZE // GROUP
        loop(0, groups, block)
        if groups * GROUP < BASIS_SIZE:
            step(groups * GROUP, BASIS_SIZE - groups * GROUP,
                 pl.ds(groups * GROUP * BASIS_SIZE, (BASIS_SIZE - groups * GROUP) * BASIS_SIZE))

    def lift(j):
        terms = jnp.concatenate(split3(rt[...].T)[:2], axis=0)
        for blk in range(2):
            add = dot(terms, sel_t[blk])
            add = (add[0:cells] + add[cells : 2 * cells]) * DTC
            tr[blk, :, pair(j)] += add.reshape(planes, ROWS, rows_z, local)

    def give_back(j):
        return remote(tr.at[other, :, pair(j)], out.at[:, pl.ds(p * half + j * ROWS, ROWS)],
                      back_s, back_r, mate)

    def keep(j):
        return pltpu.make_async_copy(tr.at[p, :, pair(j)], out.at[:, pl.ds(p * half + j * ROWS, ROWS)],
                                     keep_sem)

    def finish(j):
        give_back(j).start()
        keep(j).start()

    def start_all(copies):
        for copy in copies:
            copy.start()

    def during(index, count, f):
        @pl.when(jnp.logical_and(index >= 0, index < count))
        def _():
            f(index)

    swap(chunks - 1, p).start()
    near = pl.ds(1, half + 2)
    pltpu.make_async_copy(f0.at[p, :, near], f0.at[p, :, near], loc_sem).wait()
    loop(0, min(LEAD, chunks), lambda i: start_all(edge1(p, turn(i))))
    swap(chunks - 2, p).start()
    for n in (1, 0):
        swap_brink(n, p).start()
    early = min(EARLY, chunks - 2)
    loop(0, early, lambda u: swap(u, p).start())

    @pl.when(is_source)
    def _():
        raw_copy.start()

    @pl.when(q == 0)
    def _():
        for zh in (zh1, zh2):
            zh[0] = jnp.zeros_like(zh[0])

    @pl.when(q == nq - 1)
    def _():
        for zh in (zh1, zh2):
            zh[1] = jnp.zeros_like(zh[1])

    lane = lax.broadcasted_iota(jnp.int32, (1, BLOCK), 1)
    lane_b, lane_c = lax.div(lane, MC), lax.rem(lane, MC)

    def low_root(x):
        return -0.5 * jnp.sqrt(x.astype(jnp.float32))

    def high_root(x, count):
        return jnp.where(x + 1 < count, -0.5 * jnp.sqrt((x + 1).astype(jnp.float32)), 0.0)

    coef[0:1] = low_root(lane_b)
    coef[1:2] = high_root(lane_b, MB)
    coef[2:3] = low_root(lane_c)
    coef[3:4] = high_root(lane_c, MC)
    wide = lax.broadcasted_iota(jnp.int32, (WIDE, BLOCK), 0)
    for j in range(levels):
        level = q * levels + j
        coef[4 + j : 5 + j] = low_root(0 * lane + level)
        coef[4 + levels + j : 5 + levels + j] = high_root(0 * lane + level, MA)
        mine = jnp.where(rank[pl.ds(level, 1), :] == wide, 1.0, 0.0)
        sel_t[j // per, :, lanes(j)] = mine.astype(jnp.bfloat16)
        sel[j // per, lanes(j), :] = mine.T.astype(jnp.bfloat16)

    clear = [jnp.where(solid[pln] != 0, 0.0, 1.0).astype(jnp.bfloat16) for pln in range(planes)]
    line = lax.broadcasted_iota(jnp.int32, (rows_y, BLOCK), 0)

    def spread(e):
        pick = jnp.where(line == grid_row(p, e), 1.0, 0.0).astype(jnp.bfloat16)
        for pln in range(planes):
            mask[pln, e] = dot(clear[pln], pick) * CFL

    loop(2, half + 2, spread)

    def advance(t):
        def arrive(i):
            u = turn(i)

            @pl.when(i == 1)
            def _():
                swap(chunks - 2, other).wait_recv()
                for n in (1, 0):
                    swap_brink(n, other).wait_recv()

            @pl.when(i < chunks - 1)
            def _():
                swap(u, other).wait_recv()

            start_all(edge1(other, u))

            @pl.when(i + LEAD < chunks)
            def _():
                start_all(edge1(p, turn(i + LEAD)))

        def slope1(i):
            u = turn(i)
            whole(xh1.at[:, :, pair(u)], x1_s, x1_r.at[u]).wait_recv()
            slopes(f0, xh1, de1, u * ROWS + 2)
            z_start(*z1(u))

        def slope2(k):
            u = late(k)
            whole(xh2.at[:, :, pair(u), :, pl.ds(0, BLOCK)], x2_s, x2_r.at[ring2(u)]).wait_recv()
            slopes(f1, xh2, de2, u * ROWS + 2)
            z_start(*z2(u))

        def move1(i):
            u = turn(i)
            z_arrived(*z1(u))
            substep(f0, xh1, zh1, f1, u * ROWS + 2)
            for n in range(2):
                @pl.when(i == n)
                def _(n=n):
                    brink(n).start()
                    if n == 1:
                        loop(early, chunks - 2, lambda u: swap(u, p).start())

            for blk in range(2):
                start_all(edge2(blk, u))
            if per > 1:
                for blk in range(2):
                    start_all(edge3(blk, u))

        def move2(k):
            u = late(k)
            for n, turn_of in enumerate((0, chunks - 2)):
                @pl.when(k == turn_of)
                def _(n=n):
                    brink(n).wait_recv()

            if per > 1:
                whole(xh2.at[:, :, pair(u), :, pl.ds(BLOCK, local - BLOCK)], x2_s, x3_r.at[ring2(u)]).wait_recv()
            z_arrived(*z2(u))
            substep(f1, xh2, zh2, tr, u * ROWS + 2)

            @pl.when(is_source)
            def _():
                take_low(u)

            as_source(lambda s, lo, hi: start_all(low_send(u, s, o) for o in others(s)))

            @pl.when(jnp.logical_not(is_source))
            def _():
                finish(u)

        def meet(k):
            j = late(k)

            def one(s, lo, hi):
                if ns > 1:
                    rows = sum(spans[o][1] - spans[o][0] for o in others(s))
                    whole(lx.at[pl.ds(0, rows)], low_s, meet_r.at[ring(j)]).wait_recv()
                collide(j, s, lo, hi)
                lift(j)
                finish(j)

            as_source(one)

        during(t, chunks, arrive)
        during(t - 1, chunks, slope1)
        during(t - 2, chunks, move1)
        during(t - 4, chunks, slope2)
        during(t - 5, chunks, move2)
        @pl.when(jnp.logical_and(is_source, t == 6))
        def _():
            raw_copy.wait()

        during(t - 6, chunks, meet)

    loop(0, chunks + 6, advance)

    whole(f0.at[p, :, near], swap_s, swap_s).wait_send()
    whole(xh1.at[:, :, pl.ds(2, half)], x1_s, x1_s).wait_send()
    whole(f1.at[:, :, pl.ds(2, 2)], brink_s, brink_s).wait_send()
    whole(xh2.at[:, :, pl.ds(2, half)], x2_s, x2_s).wait_send()
    z_sent(de1, z1_s, pl.ds(2, half))
    z_sent(de2, z2_s, pl.ds(2, half))
    if ns > 1:
        as_source(lambda s, lo, hi: whole(
            lr.at[:, pl.ds(0, ns - 1), pl.ds(0, hi - lo)], low_s, low_s).wait_send())

    pltpu.make_async_copy(tr.at[p, :, pl.ds(2, half)], tr.at[p, :, pl.ds(2, half)], keep_sem).wait()
    whole(tr.at[other, :, pl.ds(2, half)], back_s, back_s).wait_send()
    whole(out.at[:, pl.ds(other * half, half)], back_r, back_r).wait_recv()


def body(hermite_coefficient_array, encounter_kernel_array, obstacle_indicator):
    planes, rows_y, rows_z, local = hermite_coefficient_array.shape
    nc = lax.axis_size("cells")
    nm = lax.axis_size("modes")
    per = local // BLOCK
    levels = 2 * per
    half = rows_y // 2
    ns = -(-(LDEG + 1) // levels)
    chunks = half // ROWS
    ext = half + 4

    index = np.arange(MODES)
    flags = (index // BLOCK + index // MC % MB + index % MC <= LDEG).astype(np.int32)
    rank = jnp.asarray(np.where(flags == 1, np.cumsum(flags) - 1, -1).reshape(MA, BLOCK), jnp.int32)

    marks = [int(flags[: min(s * levels, MA) * BLOCK].sum()) for s in range(ns + 1)]
    spans = [(lo // 16 * 16, min(-(-hi // 16) * 16, BASIS_SIZE)) for lo, hi in zip(marks[:-1], marks[1:])]
    cells = planes * ROWS * rows_z
    field = pltpu.VMEM((2, planes, ext, rows_z, local), jnp.float32)
    halo = pltpu.VMEM((2, 2, ext, rows_z, local), jnp.float32)
    slope = pltpu.VMEM((2, planes, ext, rows_z, BLOCK), jnp.float32)
    dma = pltpu.SemaphoreType.DMA
    cfg = (planes, rows_y, rows_z, local, nc, nm, spans)
    vmem = pl.BlockSpec(memory_space=pltpu.VMEM)
    anywhere = pl.BlockSpec(memory_space=pl.ANY)
    return pl.pallas_call(
        functools.partial(kernel, cfg),
        out_shape=pltpu.VMEM(hermite_coefficient_array.shape, jnp.float32),
        in_specs=[anywhere, vmem, vmem, anywhere],
        out_specs=vmem,
        scratch_shapes=[
            field, field, field, halo, halo, slope, slope, slope, slope,
            pltpu.VMEM((planes, ext, rows_z, BLOCK), jnp.float32),
            pltpu.VMEM((4 + 2 * levels + -(4 + 2 * levels) % 8, BLOCK), jnp.float32),
            pltpu.VMEM((2, local, WIDE), jnp.bfloat16),
            pltpu.VMEM((2, WIDE, local), jnp.bfloat16),
            pltpu.VMEM((chunks * WIDE, cells), jnp.float32),
            pltpu.VMEM((chunks, ns, max(hi - lo for lo, hi in spans), cells), jnp.float32),
            pltpu.VMEM((BASIS_SIZE, BASIS_SIZE * BASIS_SIZE), jnp.bfloat16),
            pltpu.VMEM((WIDE, cells), jnp.float32),
            pltpu.VMEM((WIDE, cells), jnp.float32),
            dma, dma, dma, dma((chunks + 2,)), dma, dma((chunks,)), dma, dma((RING + 1,)), dma((RING + 1,)),
            dma, dma((RING,)), dma, dma((RING,)), dma, dma((RING,)), dma, dma((2,)), dma, dma, dma,
        ],
        compiler_params=pltpu.CompilerParams(
            collective_id=0, has_side_effects=True, vmem_limit_bytes=54 * 1024 * 1024
        ),
    )(hermite_coefficient_array, obstacle_indicator.transpose(0, 2, 1), rank, encounter_kernel_array.T)


def solution(mesh):
    placed = (P("cells", None, None, "modes"), P(), P("cells", None, None))
    return jax.shard_map(
        body, mesh=mesh, in_specs=placed, out_specs=P("cells", None, None, "modes"), check_vma=False
    )
```

```python
import functools
import math

import jax
import jax.numpy as jnp
import numpy as np
from jax import lax
from jax.experimental import pallas as pl
from jax.experimental.pallas import tpu as pltpu
from jax.sharding import PartitionSpec as P

MA = 16
MB = 16
MC = 8
LDEG = 7
BASIS_SIZE = 120
MODES = 2048
BLOCK = MB * MC
WIDE = 128
GROUP = 64
ROWS = 2
LEAD = 8
RING = 8
EARLY = 6

CFL = 0.04
DTC = 0.2
MESH = pl.DeviceIdType.MESH


def split3(x):
    hi = x.astype(jnp.bfloat16)
    rest = x - hi.astype(jnp.float32)
    mid = rest.astype(jnp.bfloat16)
    low = (rest - mid.astype(jnp.float32)).astype(jnp.bfloat16)
    return hi, mid, low


def dot(a, b):
    return jnp.dot(a, b, preferred_element_type=jnp.float32)


def loop(lo, hi, f):
    def step(i, carry):
        f(i)
        return carry

    lax.fori_loop(lo, hi, step, 0)


def kernel(cfg, hin, solid, rank, raw, out, f0, f1, tr, xh1, xh2, zh1, zh2, de1, de2,
           mask, coef, sel, sel_t, lx, lr, table, lt, rt, raw_sem, loc_sem, swap_s, swap_r,
           x1_s, x1_r, x2_s, x2_r, x3_r, z1_s, z1_r, z2_s, z2_r, low_s, meet_r, brink_s, brink_r, back_s, back_r, keep_sem):
    planes, rows_y, rows_z, local, nc, nm, spans = cfg
    ns = len(spans)
    per = local // BLOCK
    levels = 2 * per
    half = rows_y // 2
    ext = half + 4
    nq = nm // 2
    chunks = half // ROWS
    cells = planes * ROWS * rows_z

    c = lax.axis_index("cells")
    m = lax.axis_index("modes")
    p = lax.rem(m, 2)
    q = lax.div(m, 2)
    other = 1 - p
    mate = (c, q * 2 + other)
    before = (lax.rem(c + nc - 1, nc), m)
    after = (lax.rem(c + 1, nc), m)
    below = (c, m - 2)
    above = (c, m + 2)
    has_below = q > 0
    has_above = q < nq - 1
    is_source = q < ns

    def peer(d):
        return (c, lax.rem(q + d, ns) * 2 + p)

    barrier = pltpu.get_barrier_semaphore()

    def greet(dev):
        pl.semaphore_signal(barrier, inc=1, device_id=dev, device_id_type=MESH)

    for dev in (mate, before, after):
        greet(dev)

    @pl.when(has_below)
    def _():
        greet(below)

    @pl.when(has_above)
    def _():
        greet(above)

    @pl.when(is_source)
    def _():
        for d in range(1, ns):
            greet(peer(d))

    def grid_row(side, e):
        return lax.rem(side * half + (rows_y - 2) + e, rows_y)

    own_pieces = [(1, 2), (2, half + 2), (half + 2, half + 3)]

    def own(i):
        lo, hi = own_pieces[i]
        return pltpu.make_async_copy(
            hin.at[:, pl.ds(grid_row(p, lo), hi - lo)],
            f0.at[p, :, pl.ds(lo, hi - lo)],
            loc_sem,
        )

    for i in range(len(own_pieces)):
        own(i).start()
    raw_copy = pltpu.make_async_copy(raw, table, raw_sem)

    greeted = 3 + has_below.astype(jnp.int32) + has_above.astype(jnp.int32)
    pl.semaphore_wait(barrier, greeted + (ns - 1) * is_source.astype(jnp.int32))

    def remote(src, dst, s, r, dev):
        return pltpu.make_async_remote_copy(
            src_ref=src, dst_ref=dst, send_sem=s, recv_sem=r, device_id=dev, device_id_type=MESH
        )

    brinks = (1, half + 2)

    def pair(u):
        return pl.ds(u * ROWS + 2, ROWS)

    def turn(i):
        return lax.rem(i + chunks - 1, chunks)

    def late(k):
        return k + lax.div(k, chunks - 2) * (2 * chunks - 3 - 2 * k)

    def ring(u):
        return lax.rem(u, RING)

    def ring2(u):
        return lax.rem(u, RING) + lax.div(u, chunks - 1) * (RING - (chunks - 1) % RING)

    def swap(u, who):
        return remote(hin.at[:, pl.ds(grid_row(other, u * ROWS + 2), ROWS)], f0.at[who, :, pair(u)],
                      swap_s, swap_r.at[u], mate)

    def swap_brink(n, who):
        return remote(hin.at[:, pl.ds(grid_row(other, brinks[n]), 1)], f0.at[who, :, pl.ds(brinks[n], 1)],
                      swap_s, swap_r.at[chunks + n], mate)

    def brink(n):
        return remote(f1.at[:, :, pl.ds((half + 1, 2)[n], 1)], f1.at[:, :, pl.ds(brinks[n], 1)],
                      brink_s, brink_r.at[n], mate)

    def edge(field, halo, ss, rs, blk, k, where, span):
        up = remote(field.at[blk, planes - 1, where, :, span], halo.at[0, blk, where, :, span], ss, rs.at[k], after)
        down = remote(field.at[blk, 0, where, :, span], halo.at[1, blk, where, :, span], ss, rs.at[k], before)
        return up, down

    def edge1(blk, u):
        return edge(f0, xh1, x1_s, x1_r, blk, u, pair(u), pl.ds(0, local))

    def edge2(blk, u):
        return edge(f1, xh2, x2_s, x2_r, blk, ring2(u), pair(u), pl.ds((local - BLOCK) * blk, BLOCK))

    def edge3(blk, u):
        return edge(f1, xh2, x2_s, x3_r, blk, ring2(u), pair(u), pl.ds(BLOCK * (1 - blk), local - BLOCK))

    def whole(ref, s, r):
        return remote(ref, ref, s, r, mate)

    def lanes(j):
        return pl.ds((j % per) * BLOCK, BLOCK)

    def gradient(field, halo, pln, e, j):
        blk = j // per
        nxt = halo[1, blk, e, :, lanes(j)] if pln == planes - 1 else field[blk, pln + 1, e, :, lanes(j)]
        prv = halo[0, blk, e, :, lanes(j)] if pln == 0 else field[blk, pln - 1, e, :, lanes(j)]
        return nxt, prv

    def slopes(field, halo, de, lo):
        def row(r):
            e = lo + r
            for pln in range(planes):
                nxt, prv = gradient(field, halo, pln, e, 0)
                de[0, pln, e] = nxt - prv
                nxt, prv = gradient(field, halo, pln, e, levels - 1)
                de[1, pln, e] = nxt - prv

        loop(0, ROWS, row)

    def to_below(de, zh, ss, rs, k, where):
        return remote(de.at[0, :, where], zh.at[1, :, where], ss, rs.at[k], below)

    def to_above(de, zh, ss, rs, k, where):
        return remote(de.at[1, :, where], zh.at[0, :, where], ss, rs.at[k], above)

    def z_start(*a):
        @pl.when(has_below)
        def _():
            to_below(*a).start()

        @pl.when(has_above)
        def _():
            to_above(*a).start()

    inner = jnp.logical_and(has_below, has_above)
    outer = jnp.logical_xor(has_below, has_above)

    def z_arrived(de, zh, ss, rs, k, where):
        @pl.when(inner)
        def _():
            whole(zh.at[:, :, where], ss, rs.at[k]).wait_recv()

        @pl.when(outer)
        def _():
            whole(zh.at[0, :, where], ss, rs.at[k]).wait_recv()

    def z_sent(de, ss, where):
        @pl.when(inner)
        def _():
            whole(de.at[:, :, where], ss, ss).wait_send()

        @pl.when(outer)
        def _():
            whole(de.at[0, :, where], ss, ss).wait_send()

    def z1(u):
        return de1, zh1, z1_s, z1_r, ring(u), pair(u)

    def z2(u):
        return de2, zh2, z2_s, z2_r, ring(u), pair(u)

    wx = 0.5 * 2.0 * math.sqrt(MA)
    wy = 0.5 * 2.0 * math.sqrt(MB)
    wz = 0.5 * 2.0 * math.sqrt(MC)
    wc = 2.0 * (wx + wy + wz)

    def substep(field, halo, zh, dest, lo):
        def row(r):
            e = lo + r
            for pln in range(planes):
                gas = mask[pln, e]
                pairs = [gradient(field, halo, pln, e, j) for j in range(levels)]
                grads = [zh[0, pln, e]] + [a - b for a, b in pairs] + [zh[1, pln, e]]
                for j in range(levels):
                    blk = j // per
                    mid = field[blk, pln, e, :, lanes(j)]
                    ny = field[blk, pln, e + 1, :, lanes(j)]
                    py = field[blk, pln, e - 1, :, lanes(j)]
                    nz = pltpu.roll(mid, rows_z - 1, 0)
                    pz = pltpu.roll(mid, 1, 0)
                    dy = ny - py
                    dz = nz - pz
                    acc = coef[4 + j : 5 + j, :] * grads[j]
                    acc += coef[4 + levels + j : 5 + levels + j, :] * grads[j + 2]
                    acc += coef[0:1, :] * pltpu.roll(dy, MC, 1)
                    acc += coef[1:2, :] * pltpu.roll(dy, BLOCK - MC, 1)
                    acc += coef[2:3, :] * pltpu.roll(dz, 1, 1)
                    acc += coef[3:4, :] * pltpu.roll(dz, BLOCK - 1, 1)
                    acc += wx * (pairs[j][0] + pairs[j][1]) + wy * (ny + py) + wz * (nz + pz) - wc * mid
                    dest[blk, pln, e, :, lanes(j)] = mid + gas * acc

        loop(0, ROWS, row)

    def slot(j):
        return pl.ds(pl.multiple_of(j * WIDE, WIDE), WIDE)

    def take_low(j):
        total = jnp.zeros((3 * cells, WIDE), jnp.float32)
        for blk in range(2):
            x = tr[blk, :, pair(j)].reshape(cells, local)
            total += dot(jnp.concatenate(split3(x), axis=0), sel[blk])
        total = total[0:cells] + total[cells : 2 * cells] + total[2 * cells : 3 * cells]
        lx[slot(j), :] = total.T

    def as_source(f):
        for s, (lo, hi) in enumerate(spans):
            pl.when(q == s)(functools.partial(f, s, lo, hi))

    def low_send(j, s, o):
        lo, hi = spans[s]
        return remote(lx.at[pl.ds(pl.multiple_of(j * WIDE + lo, 8), hi - lo)], lr.at[j, s, pl.ds(0, hi - lo)], low_s, meet_r.at[ring(j)],
                      (c, o * 2 + p))

    def others(s):
        return [o for o in range(ns) if o != s]

    def collide(j, s, lo, hi):
        lt[...] = lx[slot(j), :]
        for o in others(s):
            first_rank, last_rank = spans[o]
            lt[first_rank:last_rank, :] += lr[j, o, 0 : last_rank - first_rank]
        rt[...] = jnp.zeros_like(rt)

        def step(start, count, columns):
            rows = lt[pl.ds(start, count), :]
            values = lt[0:BASIS_SIZE, :]
            factors = jnp.concatenate(
                [(rows[i : i + 1, :] * values) for i in range(count)], axis=0
            ).astype(jnp.bfloat16)
            rt[lo:hi, :] += dot(table[lo:hi, columns], factors)

        def block(g):
            width = GROUP * BASIS_SIZE
            step(pl.multiple_of(g * GROUP, GROUP), GROUP, pl.ds(pl.multiple_of(g * width, WIDE), width))

        groups = BASIS_SIZE // GROUP
        loop(0, groups, block)
        if groups * GROUP < BASIS_SIZE:
            step(groups * GROUP, BASIS_SIZE - groups * GROUP,
                 pl.ds(groups * GROUP * BASIS_SIZE, (BASIS_SIZE - groups * GROUP) * BASIS_SIZE))

    def lift(j):
        terms = jnp.concatenate(split3(rt[...].T)[:2], axis=0)
        for blk in range(2):
            add = dot(terms, sel_t[blk])
            add = (add[0:cells] + add[cells : 2 * cells]) * DTC
            tr[blk, :, pair(j)] += add.reshape(planes, ROWS, rows_z, local)

    def give_back(j):
        return remote(tr.at[other, :, pair(j)], out.at[:, pl.ds(p * half + j * ROWS, ROWS)],
                      back_s, back_r, mate)

    def keep(j):
        return pltpu.make_async_copy(tr.at[p, :, pair(j)], out.at[:, pl.ds(p * half + j * ROWS, ROWS)],
                                     keep_sem)

    def finish(j):
        give_back(j).start()
        keep(j).start()

    def start_all(copies):
        for copy in copies:
            copy.start()

    def during(index, count, f):
        @pl.when(jnp.logical_and(index >= 0, index < count))
        def _():
            f(index)

    swap(chunks - 1, p).start()
    near = pl.ds(1, half + 2)
    pltpu.make_async_copy(f0.at[p, :, near], f0.at[p, :, near], loc_sem).wait()
    loop(0, min(LEAD, chunks), lambda i: start_all(edge1(p, turn(i))))
    swap(chunks - 2, p).start()
    for n in (1, 0):
        swap_brink(n, p).start()
    early = min(EARLY, chunks - 2)
    loop(0, early, lambda u: swap(u, p).start())

    @pl.when(is_source)
    def _():
        raw_copy.start()

    @pl.when(q == 0)
    def _():
        for zh in (zh1, zh2):
            zh[0] = jnp.zeros_like(zh[0])

    @pl.when(q == nq - 1)
    def _():
        for zh in (zh1, zh2):
            zh[1] = jnp.zeros_like(zh[1])

    lane = lax.broadcasted_iota(jnp.int32, (1, BLOCK), 1)
    lane_b, lane_c = lax.div(lane, MC), lax.rem(lane, MC)

    def low_root(x):
        return -0.5 * jnp.sqrt(x.astype(jnp.float32))

    def high_root(x, count):
        return jnp.where(x + 1 < count, -0.5 * jnp.sqrt((x + 1).astype(jnp.float32)), 0.0)

    coef[0:1] = low_root(lane_b)
    coef[1:2] = high_root(lane_b, MB)
    coef[2:3] = low_root(lane_c)
    coef[3:4] = high_root(lane_c, MC)
    wide = lax.broadcasted_iota(jnp.int32, (WIDE, BLOCK), 0)
    for j in range(levels):
        level = q * levels + j
        coef[4 + j : 5 + j] = low_root(0 * lane + level)
        coef[4 + levels + j : 5 + levels + j] = high_root(0 * lane + level, MA)
        mine = jnp.where(rank[pl.ds(level, 1), :] == wide, 1.0, 0.0)
        sel_t[j // per, :, lanes(j)] = mine.astype(jnp.bfloat16)
        sel[j // per, lanes(j), :] = mine.T.astype(jnp.bfloat16)

    clear = [jnp.where(solid[pln] != 0, 0.0, 1.0).astype(jnp.bfloat16) for pln in range(planes)]
    line = lax.broadcasted_iota(jnp.int32, (rows_y, BLOCK), 0)

    def spread(e):
        pick = jnp.where(line == grid_row(p, e), 1.0, 0.0).astype(jnp.bfloat16)
        for pln in range(planes):
            mask[pln, e] = dot(clear[pln], pick) * CFL

    loop(2, half + 2, spread)

    def advance(t):
        def arrive(i):
            u = turn(i)

            @pl.when(i == 1)
            def _():
                swap(chunks - 2, other).wait_recv()
                for n in (1, 0):
                    swap_brink(n, other).wait_recv()

            @pl.when(i < chunks - 1)
            def _():
                swap(u, other).wait_recv()

            start_all(edge1(other, u))

            @pl.when(i + LEAD < chunks)
            def _():
                start_all(edge1(p, turn(i + LEAD)))

        def slope1(i):
            u = turn(i)
            whole(xh1.at[:, :, pair(u)], x1_s, x1_r.at[u]).wait_recv()
            slopes(f0, xh1, de1, u * ROWS + 2)
            z_start(*z1(u))

        def slope2(k):
            u = late(k)
            whole(xh2.at[:, :, pair(u), :, pl.ds(0, BLOCK)], x2_s, x2_r.at[ring2(u)]).wait_recv()
            slopes(f1, xh2, de2, u * ROWS + 2)
            z_start(*z2(u))

        def move1(i):
            u = turn(i)
            z_arrived(*z1(u))
            substep(f0, xh1, zh1, f1, u * ROWS + 2)
            for n in range(2):
                @pl.when(i == n)
                def _(n=n):
                    brink(n).start()
                    if n == 1:
                        loop(early, chunks - 2, lambda u: swap(u, p).start())

            for blk in range(2):
                start_all(edge2(blk, u))
            if per > 1:
                for blk in range(2):
                    start_all(edge3(blk, u))

        def move2(k):
            u = late(k)
            for n, turn_of in enumerate((0, chunks - 2)):
                @pl.when(k == turn_of)
                def _(n=n):
                    brink(n).wait_recv()

            if per > 1:
                whole(xh2.at[:, :, pair(u), :, pl.ds(BLOCK, local - BLOCK)], x2_s, x3_r.at[ring2(u)]).wait_recv()
            z_arrived(*z2(u))
            substep(f1, xh2, zh2, tr, u * ROWS + 2)

            @pl.when(is_source)
            def _():
                take_low(u)

            as_source(lambda s, lo, hi: start_all(low_send(u, s, o) for o in others(s)))

            @pl.when(jnp.logical_not(is_source))
            def _():
                finish(u)

        def meet(k):
            j = late(k)

            def one(s, lo, hi):
                if ns > 1:
                    rows = sum(spans[o][1] - spans[o][0] for o in others(s))
                    whole(lx.at[pl.ds(0, rows)], low_s, meet_r.at[ring(j)]).wait_recv()
                collide(j, s, lo, hi)
                lift(j)
                finish(j)

            as_source(one)

        during(t, chunks, arrive)
        during(t - 1, chunks, slope1)
        during(t - 2, chunks, move1)
        during(t - 4, chunks, slope2)
        during(t - 5, chunks, move2)
        @pl.when(jnp.logical_and(is_source, t == 6))
        def _():
            raw_copy.wait()

        during(t - 6, chunks, meet)

    loop(0, chunks + 6, advance)

    whole(f0.at[p, :, near], swap_s, swap_s).wait_send()
    whole(xh1.at[:, :, pl.ds(2, half)], x1_s, x1_s).wait_send()
    whole(f1.at[:, :, pl.ds(2, 2)], brink_s, brink_s).wait_send()
    whole(xh2.at[:, :, pl.ds(2, half)], x2_s, x2_s).wait_send()
    z_sent(de1, z1_s, pl.ds(2, half))
    z_sent(de2, z2_s, pl.ds(2, half))
    if ns > 1:
        as_source(lambda s, lo, hi: whole(
            lr.at[:, pl.ds(0, ns - 1), pl.ds(0, hi - lo)], low_s, low_s).wait_send())

    pltpu.make_async_copy(tr.at[p, :, pl.ds(2, half)], tr.at[p, :, pl.ds(2, half)], keep_sem).wait()
    whole(tr.at[other, :, pl.ds(2, half)], back_s, back_s).wait_send()
    whole(out.at[:, pl.ds(other * half, half)], back_r, back_r).wait_recv()


def body(hermite_coefficient_array, encounter_kernel_array, obstacle_indicator):
    planes, rows_y, rows_z, local = hermite_coefficient_array.shape
    nc = lax.axis_size("cells")
    nm = lax.axis_size("modes")
    per = local // BLOCK
    levels = 2 * per
    half = rows_y // 2
    ns = -(-(LDEG + 1) // levels)
    chunks = half // ROWS
    ext = half + 4

    index = np.arange(MODES)
    flags = (index // BLOCK + index // MC % MB + index % MC <= LDEG).astype(np.int32)
    rank = jnp.asarray(np.where(flags == 1, np.cumsum(flags) - 1, -1).reshape(MA, BLOCK), jnp.int32)

    marks = [int(flags[: min(s * levels, MA) * BLOCK].sum()) for s in range(ns + 1)]
    spans = [(lo // 16 * 16, min(-(-hi // 8) * 8, BASIS_SIZE)) for lo, hi in zip(marks[:-1], marks[1:])]
    cells = planes * ROWS * rows_z
    field = pltpu.VMEM((2, planes, ext, rows_z, local), jnp.float32)
    halo = pltpu.VMEM((2, 2, ext, rows_z, local), jnp.float32)
    slope = pltpu.VMEM((2, planes, ext, rows_z, BLOCK), jnp.float32)
    dma = pltpu.SemaphoreType.DMA
    cfg = (planes, rows_y, rows_z, local, nc, nm, spans)
    vmem = pl.BlockSpec(memory_space=pltpu.VMEM)
    anywhere = pl.BlockSpec(memory_space=pl.ANY)
    return pl.pallas_call(
        functools.partial(kernel, cfg),
        out_shape=pltpu.VMEM(hermite_coefficient_array.shape, jnp.float32),
        in_specs=[anywhere, vmem, vmem, anywhere],
        out_specs=vmem,
        scratch_shapes=[
            field, field, field, halo, halo, slope, slope, slope, slope,
            pltpu.VMEM((planes, ext, rows_z, BLOCK), jnp.float32),
            pltpu.VMEM((4 + 2 * levels + -(4 + 2 * levels) % 8, BLOCK), jnp.float32),
            pltpu.VMEM((2, local, WIDE), jnp.bfloat16),
            pltpu.VMEM((2, WIDE, local), jnp.bfloat16),
            pltpu.VMEM((chunks * WIDE, cells), jnp.float32),
            pltpu.VMEM((chunks, ns, max(hi - lo for lo, hi in spans), cells), jnp.float32),
            pltpu.VMEM((BASIS_SIZE, BASIS_SIZE * BASIS_SIZE), jnp.bfloat16),
            pltpu.VMEM((WIDE, cells), jnp.float32),
            pltpu.VMEM((WIDE, cells), jnp.float32),
            dma, dma, dma, dma((chunks + 2,)), dma, dma((chunks,)), dma, dma((RING + 1,)), dma((RING + 1,)),
            dma, dma((RING,)), dma, dma((RING,)), dma, dma((RING,)), dma, dma((2,)), dma, dma, dma,
        ],
        compiler_params=pltpu.CompilerParams(
            collective_id=0, has_side_effects=True, vmem_limit_bytes=54 * 1024 * 1024
        ),
    )(hermite_coefficient_array, obstacle_indicator.transpose(0, 2, 1), rank, encounter_kernel_array.T)


def solution(mesh):
    placed = (P("cells", None, None, "modes"), P(), P("cells", None, None))
    return jax.shard_map(
        body, mesh=mesh, in_specs=placed, out_specs=P("cells", None, None, "modes"), check_vma=False
    )
```
